256 devices in a mesh: dom: 32 (over y, x, core), band: 8 (over z).
Axes of the slice: x: 4, y: 4, z: 8, core: 2. Of those that a mesh axis runs over, the one named last changes fastest.
Arguments:
- orbitals: bfloat16 [768, 32, 6, 1152], P('band', 'dom'), may hold values from -6 to 6
- occupations: float32 [768], P('band'), may hold values from 0.2 to 2
- previous: float32 [32, 12, 4608], P('dom'), may hold values from -6 to 6
- compensation: float32 [32, 12, 4608], P('dom'), may hold values from 0 to 1.5
- local_potential: float32 [32, 6, 1152], P('dom'), may hold values from -6 to 6
Outputs:
- applied: bfloat16 [768, 32, 6, 1152], P('band', 'dom')
- potential: float32 [32, 12, 4608], P('dom')
The draws below stay inside these ranges and needn't reach their ends.
All inputs are finite; a program needn't handle non-finite values.
Results may differ from the reference program's by a relative error of at most 0.001.
Values may be sent and summed in bfloat16 or wider, within the bound.
A program may use at most 64 MiB of HBM per device.

```python
import math
import jax
import jax.numpy as jnp
from jax import lax

BANDS = 768
BX = 6
BY = 24
BZ = 48
SWEEPS = 4
DZ = 2
DY = 4
DX = 4
N_DOM = 32


def block_scale(key, extent, pieces, least, high):
    gain, own = 1.0, jax.random.fold_in(key, 6)
    for position, blocks in pieces:
        heights = jnp.exp(jax.random.uniform(jax.random.fold_in(own, position), (blocks,), jnp.float32, least / len(pieces), high / len(pieces)))
        gain = gain * jnp.repeat(heights, extent[position] // blocks).reshape([-1 if axis == position else 1 for axis in range(len(extent))])
    return gain


def normal_values(own_key, shape, deviation, bound, pieces=(), dtype=jnp.bfloat16):
    drawn = jax.random.normal(own_key, shape, jnp.float32) * deviation
    if len(pieces) > 0:
        drawn = block_scale(own_key, shape, pieces, -0.22, 0.18) * drawn
    return jnp.clip(drawn, min=-bound, max=bound).astype(dtype)


def setup_inputs(seed: int = 0) -> dict:
    splits = jax.random.split(jax.random.key(seed), 6)
    orbitals = normal_values(splits[0], (BANDS, N_DOM, BX, BY * BZ), 1.0, 6.0, ((0, 8), (1, 32)))
    occupations = jnp.clip(jnp.exp(math.log(2.0) - 2.3025851 * jax.random.uniform(splits[1], (BANDS,), jnp.float32) ** block_scale(splits[1], (BANDS,), ((0, 8),), -0.2, 0.2)), 0.2, 2.0)
    previous = normal_values(splits[2], (N_DOM, 2 * BX, 4 * BY * BZ), 1.0, 6.0, ((0, 32),), jnp.float32)
    compensation = jnp.clip(1.5 * jax.random.uniform(splits[3], (N_DOM, 2 * BX, 4 * BY * BZ), jnp.float32) ** block_scale(splits[3], (N_DOM, 2 * BX, 4 * BY * BZ), ((0, 32),), -0.2, 0.2), 0.0, 1.5)
    local_potential = normal_values(splits[4], (N_DOM, BX, BY * BZ), 1.0, 6.0, ((0, 32),), jnp.float32)
    return dict(orbitals=orbitals, occupations=occupations, previous=previous, compensation=compensation, local_potential=local_potential)


precise = lax.Precision.HIGHEST


def to_grid(blocks, size_x, size_y, size_z):
    leading = blocks.shape[:-3]
    count = len(leading)
    shaped = blocks.reshape(leading + (DX, DY, DZ, size_x, size_y, size_z))
    permuted = tuple(range(count)) + (count, count + 3, count + 1, count + 4, count + 2, count + 5)
    return shaped.transpose(permuted).reshape(leading + (DX * size_x, DY * size_y, DZ * size_z))


def to_blocks(grid_field, size_x, size_y, size_z):
    leading = grid_field.shape[:-3]
    count = len(leading)
    shaped = grid_field.reshape(leading + (DX, size_x, DY, size_y, DZ, size_z))
    permuted = tuple(range(count)) + (count, count + 2, count + 4, count + 1, count + 3, count + 5)
    return shaped.transpose(permuted).reshape(leading + (DX * DY * DZ, size_x, size_y * size_z))


def pad_three(array_in):
    return jnp.pad(array_in, [(0, 0)] * (array_in.ndim - 3) + [(1, 1)] * 3)


def neighbour_sum(array_in):
    padded = pad_three(array_in)
    total = padded[..., 2:, 1:-1, 1:-1] + padded[..., :-2, 1:-1, 1:-1]
    total = total + padded[..., 1:-1, 2:, 1:-1] + padded[..., 1:-1, :-2, 1:-1]
    return total + padded[..., 1:-1, 1:-1, 2:] + padded[..., 1:-1, 1:-1, :-2]


def refine_axis(padded, along):
    front = jnp.moveaxis(padded, along, 0)
    middle = front[1:-1]
    even_rows = 0.75 * middle + 0.25 * front[:-2]
    odd_rows = 0.75 * middle + 0.25 * front[2:]
    refined = jnp.stack([even_rows, odd_rows], 1).reshape((2 * middle.shape[0],) + middle.shape[1:])
    return jnp.moveaxis(refined, 0, along)


def coarsen_axis(padded, along):
    front = jnp.moveaxis(padded, along, 0)
    half_rows = (front.shape[0] - 2) // 2
    middle = front[1:-1].reshape((half_rows, 2) + front.shape[1:])
    left_rows = front[0:2 * half_rows:2]
    right_rows = front[3:2 * half_rows + 2:2]
    coarse = 0.5 * (0.25 * left_rows + 0.75 * middle[:, 0] + 0.75 * middle[:, 1] + 0.25 * right_rows)
    return jnp.moveaxis(coarse, 0, along)


def reference(orbitals, occupations, previous, compensation, local_potential):
    group_size = math.gcd(BANDS, 32)
    orbital_groups = orbitals.reshape(BANDS // group_size, group_size, N_DOM, BX, BY * BZ)
    occupation_groups = occupations.reshape(BANDS // group_size, group_size)

    def accumulate(running, items):
        wave_field = items[0].astype(jnp.float32).reshape(group_size, N_DOM * BX * BY * BZ)
        return running + jnp.dot(items[1], wave_field * wave_field, precision=precise), None

    running, unused = lax.scan(accumulate, jnp.zeros((N_DOM * BX * BY * BZ,), jnp.float32), (orbital_groups, occupation_groups))
    density = to_grid((running / BANDS).reshape(N_DOM, BX, BY * BZ), BX, BY, BZ)
    refined = refine_axis(pad_three(density), 0)
    refined = refine_axis(refined, 1)
    refined = refine_axis(refined, 2)
    source = math.pi * (refined - to_grid(compensation, 2 * BX, 2 * BY, 2 * BZ))
    potential = to_grid(previous, 2 * BX, 2 * BY, 2 * BZ)
    for counter in range(SWEEPS):
        potential = (neighbour_sum(potential) + source) / 6.0
    coarse = coarsen_axis(pad_three(potential), 0)
    coarse = coarsen_axis(coarse, 1)
    coarse = coarsen_axis(coarse, 2)
    effective = coarse - jnp.cbrt(3.0 / math.pi * density) + to_grid(local_potential, BX, BY, BZ)
    effective_blocks = to_blocks(effective, BX, BY, BZ)

    def apply_group(group):
        wave_field = group.astype(jnp.float32)
        grid_field = to_grid(wave_field, BX, BY, BZ)
        laplace = to_blocks(neighbour_sum(grid_field) - 6.0 * grid_field, BX, BY, BZ)
        return (-0.5 * laplace + effective_blocks[None] * wave_field).astype(jnp.bfloat16)

    applied = lax.map(apply_group, orbital_groups).reshape(BANDS, N_DOM, BX, BY * BZ)
    return applied, to_blocks(potential, 2 * BX, 2 * BY, 2 * BZ)
```

```python
import functools
import math

import jax
import jax.numpy as jnp
from jax import lax
from jax.experimental import pallas as pl
from jax.experimental.pallas import tpu as pltpu
from jax.sharding import PartitionSpec as P

BX, BY, BZ = 6, 24, 48
YZ = BY * BZ
FX, FY, FZ = 2 * BX, 2 * BY, 2 * BZ
FYZ = FY * FZ
BANDS = 768
SWEEPS = 4
M = 5
NX = FX + 2 * M
YROWS = FY + 16
EDGE = 192
OWN = FX * 36
LANES = 128
MESH = pl.DeviceIdType.MESH
F32, BF16 = jnp.float32, jnp.bfloat16
EXACT = lax.Precision.HIGHEST

OFFSETS = [
    (dx, dy, dz) for dx in (-1, 0, 1) for dy in (-1, 0, 1) for dz in (0, 1) if (dx, dy, dz) != (0, 0, 0)
]


def slot_of(dx, dy, dz):
    return ((dx + 1) * 3 + dy + 1) * 2 + dz


HALO = 0
BAND = 18
ORB_X, ORB_Y, ORB_Z = 26, 28, 30
POT_X, POT_Y, POT_Z = 31, 35, 39
N_SEM = 41


def iota(shape, axis):
    return lax.broadcasted_iota(jnp.int32, shape, axis)


def step_kernel(
    sizes,
    orb, occ_in, prev_in, comp_in, loc_in,
    stencil, eff_out, pot_out,
    obuf, zbuf, ylo, yhi, w_ref, occ, occ_col,
    pvx, cmx, send_v, send_c, edge_v, edge_c, loc,
    va, vb, sa, vz, sz,
    part, gath, tot, totb, rh, xo, xz, cbuf, f1, f2, g3, c3, tmp_m,
    load_sem, send_sem, recv_sem,
):
    nb, n_band, nx, ny = sizes
    me = lax.axis_index("dom")
    band = lax.axis_index("band")
    bi = me // (ny * 2)
    bj = (me // 2) % ny
    bk = me % 2
    has_xlo, has_xhi = bi > 0, bi < nx - 1
    has_ylo, has_yhi = bj > 0, bj < ny - 1

    def exists(dx, dy):
        ok = None
        for flag in ([has_xlo] if dx < 0 else [has_xhi] if dx > 0 else []) + (
            [has_ylo] if dy < 0 else [has_yhi] if dy > 0 else []
        ):
            ok = flag if ok is None else jnp.logical_and(ok, flag)
        return ok

    def when(cond, fn):
        if cond is None:
            fn()
        else:
            pl.when(cond)(fn)

    def neighbour(dx, dy, dz):
        other = (1 - bk) if dz else bk
        return {"dom": ((bi + dx) * ny + bj + dy) * 2 + other, "band": band}

    def remote(src, dst, s_idx, r_idx, device):
        return pltpu.make_async_remote_copy(
            src_ref=src, dst_ref=dst, send_sem=send_sem.at[s_idx], recv_sem=recv_sem.at[r_idx],
            device_id=device, device_id_type=MESH,
        )

    cp_occ = pltpu.make_async_copy(occ_in, occ, load_sem.at[BX])
    cp_prev = pltpu.make_async_copy(prev_in, pvx.at[pl.ds(EDGE, OWN)], load_sem.at[BX + 1])
    cp_comp = pltpu.make_async_copy(comp_in, cmx.at[pl.ds(EDGE, OWN)], load_sem.at[BX + 2])
    cp_loc = pltpu.make_async_copy(loc_in, loc, load_sem.at[BX + 3])
    loads = [pltpu.make_async_copy(orb.at[x], obuf.at[x + 1], load_sem.at[x]) for x in range(BX)]
    cp_occ.start()
    cp_prev.start()
    cp_comp.start()
    for cp in loads:
        cp.start()
    cp_loc.start()

    barrier = pltpu.get_barrier_semaphore()
    for d in range(1, n_band):
        pl.semaphore_signal(
            barrier, inc=1, device_id={"dom": me, "band": (band + d) % n_band}, device_id_type=MESH
        )
    for dx, dy, dz in OFFSETS:
        def greet(dx=dx, dy=dy, dz=dz):
            pl.semaphore_signal(barrier, inc=1, device_id=neighbour(dx, dy, dz), device_id_type=MESH)
        when(exists(dx, dy), greet)

    def zero(ref, *index):
        def run():
            view = ref.at[index] if index else ref
            view[...] = jnp.zeros(view.shape, view.dtype)
        return run

    when(jnp.logical_not(has_xhi), zero(obuf, BX + 1))
    when(jnp.logical_not(has_xlo), zero(obuf, 0))
    for ref in (edge_v, edge_c):
        when(jnp.logical_not(has_xhi), zero(ref, 0))
        when(jnp.logical_not(has_xlo), zero(ref, 1))
    when(jnp.logical_not(has_ylo), zero(ylo))
    when(jnp.logical_not(has_yhi), zero(yhi))
    for dx, dy, dz in OFFSETS:
        cond = exists(dx, dy)
        if cond is not None:
            when(jnp.logical_not(cond), zero(rh, slot_of(dx, dy, dz)))
    for ref in (va, sa):
        when(jnp.logical_not(has_ylo), zero(ref, slice(None), pl.ds(0, 8)))
        when(jnp.logical_not(has_yhi), zero(ref, slice(None), pl.ds(8 + FY, 8)))
    for x in (0, NX - 1):
        vb[x] = jnp.zeros((YROWS, LANES), F32)
    cbuf[...] = jnp.zeros(cbuf.shape, F32)
    xo[...] = jnp.zeros(xo.shape, F32)
    xz[...] = jnp.zeros(xz.shape, F32)

    def fill_w(r, carry):
        row = iota((LANES, 384), 0) + r * LANES
        col = iota((LANES, 384), 1)
        place = col % BZ
        diff = row - LANES - col
        main = jnp.where(diff == 0, 3.0, 0.0)
        side = (
            (diff == BZ) | (diff == -BZ)
            | ((diff == 1) & (place != BZ - 1)) | ((diff == -1) & (place != 0))
        )
        main = jnp.where(side, -0.5, main)
        far = row - 640 - col
        over = jnp.where(
            bk == 0,
            jnp.where((far == 1 - BZ) & (place == BZ - 1), -0.5, 0.0),
            jnp.where((far == BZ - 1) & (place == 0), -0.5, 0.0),
        )
        w_ref[pl.ds(pl.multiple_of(r * LANES, LANES), LANES), :] = jnp.where(row < 640, main, over).astype(BF16)
        return carry

    lax.fori_loop(0, 8, fill_w, 0)

    cp_occ.wait()
    diagonal = jnp.where(iota((nb, nb), 0) == iota((nb, nb), 1), occ[...] * (1.0 / BANDS), 0.0)
    occ_col[...] = jnp.broadcast_to(jnp.sum(diagonal, 1, keepdims=True), (nb, LANES))

    cp_prev.wait()
    cp_comp.wait()
    send_v[...] = pvx[EDGE : EDGE + OWN, :].astype(BF16)
    send_c[...] = cmx[EDGE : EDGE + OWN, :].astype(BF16)

    one = lambda flag: jnp.where(flag, 1, 0)
    n_dom = (1 + one(has_xlo) + one(has_xhi)) * (1 + one(has_ylo) + one(has_yhi)) * 2 - 1
    pl.semaphore_wait(barrier, n_dom + n_band - 1)

    px_dn, px_up = [], []
    for n, (src, dst) in enumerate(((send_v, edge_v), (send_c, edge_c))):
        px_dn.append(remote(src.at[pl.ds(0, EDGE)], dst.at[0], POT_X + 2 * n, POT_X + 2 * n, neighbour(-1, 0, 0)))
        px_up.append(
            remote(
                src.at[pl.ds(OWN - EDGE, EDGE)], dst.at[1], POT_X + 2 * n + 1, POT_X + 2 * n + 1, neighbour(1, 0, 0)
            )
        )
    for cp in px_dn:
        when(has_xlo, cp.start)
    for cp in px_up:
        when(has_xhi, cp.start)

    oz = remote(orb, zbuf, ORB_Z, ORB_Z, neighbour(0, 0, 1))
    oz.start()
    oy_dn = remote(orb.at[:, :, pl.ds(0, LANES)], yhi, ORB_Y, ORB_Y, neighbour(0, -1, 0))
    oy_up = remote(orb.at[:, :, pl.ds(YZ - LANES, LANES)], ylo, ORB_Y + 1, ORB_Y + 1, neighbour(0, 1, 0))
    ox_dn = remote(orb.at[0], obuf.at[BX + 1], ORB_X, ORB_X, neighbour(-1, 0, 0))
    ox_up = remote(orb.at[BX - 1], obuf.at[0], ORB_X + 1, ORB_X + 1, neighbour(1, 0, 0))
    when(has_xlo, ox_dn.start)
    when(has_xhi, ox_up.start)
    when(has_ylo, oy_dn.start)
    when(has_yhi, oy_up.start)

    for x in range(BX):
        loads[x].wait()

        def body(g, acc, x=x):
            rows = pl.ds(pl.multiple_of(g * 16, 16), 16)
            share = occ_col[rows, :]
            out = []
            for blk in range(YZ // LANES):
                wave = obuf[x + 1, rows, LANES * blk : LANES * (blk + 1)].astype(F32)
                term = (wave * share) * wave
                out.append(acc[blk] + (term[0:8] + term[8:16]))
            return tuple(out)

        acc = lax.fori_loop(0, nb // 16, body, (jnp.zeros((8, LANES), F32),) * (YZ // LANES))
        for blk in range(YZ // LANES):
            part[x : x + 1, LANES * blk : LANES * (blk + 1)] = jnp.sum(acc[blk], 0, keepdims=True)
    part[BX:8, :] = jnp.zeros((8 - BX, YZ), F32)
    gath[band] = part[...].astype(BF16)
    band_copies = []
    for d in range(1, n_band):
        cp = remote(
            gath.at[band], gath.at[band], BAND + d, BAND + d, {"dom": me, "band": (band + d) % n_band}
        )
        cp.start()
        band_copies.append(cp)

    for cp in px_dn:
        when(has_xhi, cp.wait_recv)
    for cp in px_up:
        when(has_xlo, cp.wait_recv)
    for full, edge in ((pvx, edge_v), (cmx, edge_c)):
        full[EDGE + OWN : 2 * EDGE + OWN, :] = edge[0].astype(F32)
        full[0:EDGE, :] = edge[1].astype(F32)
    lane12 = iota((12, LANES), 1)

    def split(x, carry):
        base = EDGE - 36 * M + 36 * x
        for src, dst, scale in ((pvx, va, None), (cmx, sa, -math.pi)):
            a0, a1, a2 = (src[pl.ds(base + r, 12, stride=3), :] for r in range(3))
            if scale is not None:
                a0, a1, a2 = scale * a0, scale * a1, scale * a2
            cut = lane12 < FZ
            y0 = a0
            y1 = jnp.where(lane12 < 32, pltpu.roll(a0, 32, 1), pltpu.roll(a1, 32, 1))
            y2 = jnp.where(lane12 < 64, pltpu.roll(a1, 64, 1), pltpu.roll(a2, 64, 1))
            y3 = pltpu.roll(a2, 96, 1)
            for q, val in enumerate((y0, y1, y2, y3)):
                dst[x, pl.ds(8 + q, 12, stride=4), :] = jnp.where(cut, val, 0.0)
        return carry

    lax.fori_loop(0, NX, split, 0)
    y_copies = []
    for n, ref in enumerate((va, sa)):
        dn = remote(
            ref.at[:, pl.ds(8, 8)], ref.at[:, pl.ds(8 + FY, 8)], POT_Y + 2 * n, POT_Y + 2 * n, neighbour(0, -1, 0)
        )
        up = remote(
            ref.at[:, pl.ds(FY, 8)], ref.at[:, pl.ds(0, 8)], POT_Y + 2 * n + 1, POT_Y + 2 * n + 1, neighbour(0, 1, 0)
        )
        when(has_ylo, dn.start)
        when(has_yhi, up.start)
        y_copies.append((dn, up))
    for dn, up in y_copies:
        when(has_yhi, dn.wait_recv)
        when(has_ylo, up.wait_recv)
    z_copies = [
        remote(va, vz, POT_Z, POT_Z, neighbour(0, 0, 1)),
        remote(sa, sz, POT_Z + 1, POT_Z + 1, neighbour(0, 0, 1)),
    ]
    for cp in z_copies:
        cp.start()

    for cp in band_copies:
        cp.wait_recv()
    rho = gath[0].astype(F32)
    for d in range(1, n_band):
        rho = rho + gath[d].astype(F32)
    tot[...] = rho
    totb[...] = rho.astype(BF16)
    halo_copies = []
    for dx, dy, dz in OFFSETS:
        there = slot_of(-dx, -dy, dz)
        cols = {0: pl.ds(0, YZ), -1: pl.ds(0, 256), 1: pl.ds(YZ - 256, 256)}[dy]
        cp = remote(
            totb.at[:, cols], rh.at[there, :, cols], HALO + slot_of(dx, dy, dz), HALO + there,
            neighbour(dx, dy, dz),
        )
        when(exists(dx, dy), cp.start)
        halo_copies.append((dx, dy, cp))

    oz.wait_recv()
    when(has_yhi, oy_dn.wait_recv)
    when(has_ylo, oy_up.wait_recv)
    when(has_xhi, ox_dn.wait_recv)
    when(has_xlo, ox_up.wait_recv)

    def apply(x, carry):
        for t in range(3):
            if t == 0:
                here = [ylo[x], obuf[x + 1, :, 0:512]]
            elif t == 1:
                here = [obuf[x + 1, :, 256:896]]
            else:
                here = [obuf[x + 1, :, 640:1152], yhi[x]]
            lhs = jnp.concatenate([*here, zbuf[x, :, 384 * t : 384 * (t + 1)]], 1)
            out = jnp.dot(lhs, w_ref[...], preferred_element_type=F32)
            cols = slice(384 * t, 384 * (t + 1))
            sides = obuf[x, :, cols].astype(F32) + obuf[x + 2, :, cols].astype(F32)
            stencil[x, :, cols] = out - 0.5 * sides
        return carry

    lax.fori_loop(0, BX, apply, 0)

    for cp in z_copies:
        cp.wait_recv()
        cp.wait_send()
    for dn, up in y_copies:
        when(has_ylo, dn.wait_send)
        when(has_yhi, up.wait_send)
    lane = iota((YROWS, LANES), 1)
    from_z = jnp.where(bk == 0, jnp.where((lane >= FZ) & (lane < FZ + M), 1, 0), jnp.where(lane >= LANES - M, 1, 0)) == 1
    shift = FZ - 64 * bk

    def merge(x, carry):
        va[x] = jnp.where(from_z, pltpu.roll(vz[x], shift, 1), va[x])
        sa[x] = jnp.where(from_z, pltpu.roll(sz[x], shift, 1), sa[x])
        return carry

    lax.fori_loop(0, NX, merge, 0)

    for dx, dy, cp in halo_copies:
        when(exists(-dx, -dy), cp.wait_recv)
    for dst, dz in ((xo, 0), (xz, 1)):
        for dy, start, width, at in ((0, 0, YZ, 256), (-1, YZ - 256, 256, 0), (1, 0, 256, 256 + YZ)):
            cols = slice(start, start + width)
            own = tot[...] if dz == 0 and dy == 0 else rh[slot_of(0, dy, dz), :, cols].astype(F32)
            above = rh[slot_of(1, dy, dz), :, cols].astype(F32)
            below = rh[slot_of(-1, dy, dz), :, cols].astype(F32)
            lanes = slice(at, at + width)
            dst[0:3, lanes] = below[3:6]
            dst[3:9, lanes] = own[0:6]
            dst[9:12, lanes] = above[0:3]

    def split_rho(g, carry):
        window = pl.ds(pl.multiple_of(g * 384, 384), 512)
        for src, base in ((xo, 0), (xz, 64)):
            block = src[:, window]
            for q in range(8):
                cbuf[g * 8 + q, :, base : base + BZ] = block[:, 112 + BZ * q : 112 + BZ * (q + 1)]
        return carry

    lax.fori_loop(0, 4, split_rho, 0)
    source_row = iota((LANES, LANES), 0)
    fine_lane = iota((LANES, LANES), 1)
    fine_z = jnp.where(fine_lane >= LANES - M, fine_lane - LANES, fine_lane)
    coarse = jnp.where(source_row < 64, source_row, source_row - 64 + jnp.where(bk == 0, BZ, -BZ))
    real = (source_row < BZ) | ((source_row >= 64) & (source_row < 64 + BZ))
    odd = (fine_z + 128) % 2
    half = (fine_z + 128) // 2 - 64
    wz = jnp.where(coarse == half, 0.75 * math.pi, 0.0)
    wz = jnp.where(coarse == half - 1 + 2 * odd, 0.25 * math.pi, wz)
    wz = jnp.where(real, wz, 0.0)
    fine = jnp.dot(
        cbuf[...].reshape(32 * 16, LANES), wz, precision=EXACT, preferred_element_type=F32
    ).reshape(32, 16, LANES)
    for y in range(30):
        f1[pl.ds(y + 5, 12, stride=40), :] = fine[y, 0:12]

    def refine_y(x, carry):
        base = pl.multiple_of(x * 40, 8)
        block = f1[pl.ds(base, 40), :]
        mid = 0.75 * block[6:34]
        f2[x, pl.ds(4, 28, stride=2), :] = mid + 0.25 * block[5:33]
        f2[x, pl.ds(5, 28, stride=2), :] = mid + 0.25 * block[7:35]
        return carry

    lax.fori_loop(0, 12, refine_y, 0)

    def refine_x(x, carry):
        mid = 0.75 * f2[x]
        at = 2 * x - 1
        sa[at] = sa[at] + mid + 0.25 * f2[x - 1]
        sa[at + 1] = sa[at + 1] + mid + 0.25 * f2[x + 1]
        return carry

    lax.fori_loop(1, 11, refine_x, 0)

    yrow = iota((YROWS, LANES), 0)
    y_ok = ((yrow >= 8) | has_ylo) & ((yrow < 8 + FY) | has_yhi)
    z_ok = (lane < FZ) | from_z
    sixth = jnp.where(y_ok & z_ok, 1.0 / 6.0, 0.0)
    x_low = jnp.where(has_xlo, 1.0, 0.0)
    x_high = jnp.where(has_xhi, 1.0, 0.0)

    for sweep in range(SWEEPS):
        old, new = (va, vb) if sweep % 2 == 0 else (vb, va)

        def update(x, carry, old=old, new=new):
            mid = old[x]
            acc = old[x - 1] + old[x + 1] + sa[x]
            acc = acc + pltpu.roll(mid, 1, 0) + pltpu.roll(mid, YROWS - 1, 0)
            acc = acc + pltpu.roll(mid, 1, 1) + pltpu.roll(mid, LANES - 1, 1)
            factor = jnp.where(x < M, x_low, jnp.where(x >= M + FX, x_high, 1.0))
            new[x] = acc * (sixth * factor)
            return carry

        lax.fori_loop(1 + sweep, NX - 1 - sweep, update, 0)

    def coarsen(x, carry):
        at = 2 * x + M
        g3[...] = 0.125 * (va[at - 1] + va[at + 2]) + 0.375 * (va[at] + va[at + 1])
        c3[pl.ds(pl.multiple_of(x * BY, 8), BY), :] = 0.125 * (
            g3[pl.ds(7, BY, stride=2), :] + g3[pl.ds(10, BY, stride=2), :]
        ) + 0.375 * (g3[pl.ds(8, BY, stride=2), :] + g3[pl.ds(9, BY, stride=2), :])
        return carry

    lax.fori_loop(0, BX, coarsen, 0)
    lane_in = iota((LANES, LANES), 0)
    cell = iota((LANES, LANES), 1)
    rel = jnp.where(lane_in == LANES - 1, -1, lane_in) - 2 * cell
    wr = jnp.where((rel == 0) | (rel == 1), 0.375, 0.0)
    wr = jnp.where((rel == -1) | (rel == 2), 0.125, wr)
    wr = jnp.where(cell < BZ, wr, 0.0)
    c3[...] = jnp.dot(c3[...], wr, precision=EXACT, preferred_element_type=F32)
    cp_loc.wait()
    for y in range(BY):
        tmp_m[0:BX, y * BZ : (y + 1) * BZ] = c3[pl.ds(y, BX, stride=BY), :][:, 0:BZ]
    for x in range(BX):
        cube = jnp.exp(jnp.log((3.0 / math.pi) * tot[x : x + 1, :]) * (1.0 / 3.0))
        eff_out[x : x + 1, :] = (tmp_m[x : x + 1, :] - cube) + loc[x]

    def join(x, carry):
        p0, p1, p2, p3 = (va[x + M, pl.ds(8 + q, 12, stride=4), :] for q in range(4))
        r0 = jnp.where(lane12 < 96, p0, pltpu.roll(p1, 96, 1))
        r1 = jnp.where(lane12 < 64, pltpu.roll(p1, 96, 1), pltpu.roll(p2, 64, 1))
        r2 = jnp.where(lane12 < 32, pltpu.roll(p2, 64, 1), pltpu.roll(p3, 32, 1))
        for r, val in enumerate((r0, r1, r2)):
            pot_out[pl.ds(36 * x + r, 12, stride=3), :] = val
        return carry

    lax.fori_loop(0, FX, join, 0)

    for cp in px_dn:
        when(has_xlo, cp.wait_send)
    for cp in px_up:
        when(has_xhi, cp.wait_send)
    oz.wait_send()
    when(has_ylo, oy_dn.wait_send)
    when(has_yhi, oy_up.wait_send)
    when(has_xlo, ox_dn.wait_send)
    when(has_xhi, ox_up.wait_send)
    for cp in band_copies:
        cp.wait_send()
    for dx, dy, cp in halo_copies:
        when(exists(dx, dy), cp.wait_send)


def solution(mesh):
    n_band = mesh.shape["band"]
    domains = mesh.shape["dom"]
    ny = min(4, domains // 4)
    nx = domains // (ny * 2)

    def local(orbitals, occupations, previous, compensation, local_potential):
        nb = orbitals.shape[0]
        any_space = pl.BlockSpec(memory_space=pl.ANY)
        vmem = pl.BlockSpec(memory_space=pltpu.VMEM)
        waves = orbitals[:, 0].transpose(1, 0, 2)
        stencil, effective, potential = pl.pallas_call(
            functools.partial(step_kernel, (nb, n_band, nx, ny)),
            out_shape=(
                jax.ShapeDtypeStruct((BX, nb, YZ), F32),
                jax.ShapeDtypeStruct((BX, YZ), F32),
                jax.ShapeDtypeStruct((OWN, LANES), F32),
            ),
            in_specs=[any_space] * 5,
            out_specs=(vmem, vmem, vmem),
            scratch_shapes=[
                pltpu.VMEM((BX + 2, nb, YZ), BF16),
                pltpu.VMEM((BX, nb, YZ), BF16),
                pltpu.VMEM((BX, nb, LANES), BF16),
                pltpu.VMEM((BX, nb, LANES), BF16),
                pltpu.VMEM((1024, 384), BF16),
                pltpu.VMEM((1, nb), F32),
                pltpu.VMEM((nb, LANES), F32),
                pltpu.VMEM((2 * EDGE + OWN, LANES), F32),
                pltpu.VMEM((2 * EDGE + OWN, LANES), F32),
                pltpu.VMEM((OWN, LANES), BF16),
                pltpu.VMEM((OWN, LANES), BF16),
                pltpu.VMEM((2, EDGE, LANES), BF16),
                pltpu.VMEM((2, EDGE, LANES), BF16),
                pltpu.VMEM((BX, 1, YZ), F32),
            ]
            + [pltpu.VMEM((NX, YROWS, LANES), F32)] * 5
            + [
                pltpu.VMEM((8, YZ), F32),
                pltpu.VMEM((n_band, 8, YZ), BF16),
                pltpu.VMEM((8, YZ), F32),
                pltpu.VMEM((8, YZ), BF16),
                pltpu.VMEM((18, 8, YZ), BF16),
                pltpu.VMEM((16, 512 + YZ), F32),
                pltpu.VMEM((16, 512 + YZ), F32),
                pltpu.VMEM((32, 16, LANES), F32),
                pltpu.VMEM((12 * 40, LANES), F32),
                pltpu.VMEM((12, YROWS, LANES), F32),
                pltpu.VMEM((YROWS, LANES), F32),
                pltpu.VMEM((BX * BY, LANES), F32),
                pltpu.VMEM((8, YZ), F32),
                pltpu.SemaphoreType.DMA((BX + 4,)),
                pltpu.SemaphoreType.DMA((N_SEM,)),
                pltpu.SemaphoreType.DMA((N_SEM,)),
            ],
            compiler_params=pltpu.CompilerParams(
                collective_id=0, has_side_effects=True, vmem_limit_bytes=48 * 1024 * 1024
            ),
        )(
            waves,
            occupations.reshape(1, nb),
            previous.reshape(OWN, LANES),
            compensation.reshape(OWN, LANES),
            local_potential.reshape(BX, 1, YZ),
        )
        applied = (stencil + effective[:, None] * waves.astype(F32)).astype(BF16)
        return applied.transpose(1, 0, 2)[:, None], potential.reshape(previous.shape)

    return jax.shard_map(
        local,
        mesh=mesh,
        in_specs=(
            P("band", "dom", None, None),
            P("band"),
            P("dom", None, None),
            P("dom", None, None),
            P("dom", None, None),
        ),
        out_specs=(P("band", "dom", None, None), P("dom", None, None)),
        check_vma=False,
    )
```

```python
import functools
import math

import jax
import jax.numpy as jnp
from jax import lax
from jax.experimental import pallas as pl
from jax.experimental.pallas import tpu as pltpu
from jax.sharding import PartitionSpec as P

BX, BY, BZ = 6, 24, 48
YZ = BY * BZ
FX, FY, FZ = 2 * BX, 2 * BY, 2 * BZ
FYZ = FY * FZ
BANDS = 768
SWEEPS = 4
M = 5
NX = FX + 2 * M
Y0 = 16
YROWS = FY + 2 * Y0
SPAN = FY + 16
EDGE = 192
OWN = FX * 36
LANES = 128
MESH = pl.DeviceIdType.MESH
F32, BF16 = jnp.float32, jnp.bfloat16
EXACT = lax.Precision.HIGHEST

OFFSETS = [
    (dx, dy, dz) for dx in (-1, 0, 1) for dy in (-1, 0, 1) for dz in (0, 1) if (dx, dy, dz) != (0, 0, 0)
]


def slot_of(dx, dy, dz):
    return ((dx + 1) * 3 + dy + 1) * 2 + dz


HALO = 0
BAND = 18
ORB_X, ORB_Y, ORB_Z = 26, 28, 30
POT_X, POT_Y, POT_Z = 31, 35, 39
N_SEM = 41


def loop(low, high, body, together):
    def some(step, carry):
        for u in range(together):
            body(low + step * together + u)
        return carry

    assert (high - low) % together == 0
    lax.fori_loop(0, (high - low) // together, some, 0)


def iota(shape, axis):
    return lax.broadcasted_iota(jnp.int32, shape, axis)


def step_kernel(
    sizes,
    orb, occ_in, prev_in, comp_in, loc_in,
    stencil, eff_out, pot_out, waves,
    xlo, xhi, zbuf, ylo, yhi, w_ref, occ, occ_col,
    pvx, cmx, send_v, send_c, edge_v, edge_c, loc,
    va, vb, sa, rim_out, rim_in, zsend, zrecv,
    part, gath, tot, totb, rh, xo, xz, cbuf, f1, f2, g3, c3, tmp_m, base,
    load_sem, send_sem, recv_sem,
):
    nb, n_band, nx, ny = sizes
    me = lax.axis_index("dom")
    band = lax.axis_index("band")
    bi = me // (ny * 2)
    bj = (me // 2) % ny
    bk = me % 2
    has_xlo, has_xhi = bi > 0, bi < nx - 1
    has_ylo, has_yhi = bj > 0, bj < ny - 1

    def exists(dx, dy):
        ok = None
        for flag in ([has_xlo] if dx < 0 else [has_xhi] if dx > 0 else []) + (
            [has_ylo] if dy < 0 else [has_yhi] if dy > 0 else []
        ):
            ok = flag if ok is None else jnp.logical_and(ok, flag)
        return ok

    def when(cond, fn):
        if cond is None:
            fn()
        else:
            pl.when(cond)(fn)

    def neighbour(dx, dy, dz):
        other = (1 - bk) if dz else bk
        return {"dom": ((bi + dx) * ny + bj + dy) * 2 + other, "band": band}

    def remote(src, dst, s_idx, r_idx, device):
        return pltpu.make_async_remote_copy(
            src_ref=src, dst_ref=dst, send_sem=send_sem.at[s_idx], recv_sem=recv_sem.at[r_idx],
            device_id=device, device_id_type=MESH,
        )

    leftovers = []

    def send(cp, where, arrival):
        when(where, cp.start)
        handle = [cp, arrival, False]
        leftovers.append((handle, where))
        return handle

    def arrive(*handles):
        for handle in handles:
            when(handle[1], handle[0].wait_recv)
            handle[2] = True

    def finish():
        for handle, where in leftovers:
            if not handle[2]:
                arrive(handle)
            when(where, handle[0].wait_send)

    cp_occ = pltpu.make_async_copy(occ_in, occ, load_sem.at[BX])
    cp_prev = pltpu.make_async_copy(prev_in, pvx.at[pl.ds(EDGE, OWN)], load_sem.at[BX + 1])
    cp_comp = pltpu.make_async_copy(comp_in, cmx.at[pl.ds(EDGE, OWN)], load_sem.at[BX + 2])
    cp_loc = pltpu.make_async_copy(loc_in, loc, load_sem.at[BX + 3])
    loads = [pltpu.make_async_copy(orb.at[x], waves.at[x], load_sem.at[x]) for x in range(BX)]
    cp_occ.start()
    for cp in loads:
        cp.start()
    cp_prev.start()
    cp_comp.start()
    cp_loc.start()

    barrier = pltpu.get_barrier_semaphore()
    for d in range(1, n_band):
        pl.semaphore_signal(
            barrier, inc=1, device_id={"dom": me, "band": (band + d) % n_band}, device_id_type=MESH
        )
    for dx, dy, dz in OFFSETS:
        def greet(dx=dx, dy=dy, dz=dz):
            pl.semaphore_signal(barrier, inc=1, device_id=neighbour(dx, dy, dz), device_id_type=MESH)
        when(exists(dx, dy), greet)

    cp_occ.wait()
    diagonal = jnp.where(iota((nb, nb), 0) == iota((nb, nb), 1), occ[...] * (1.0 / BANDS), 0.0)
    occ_col[...] = jnp.broadcast_to(jnp.sum(diagonal, 1, keepdims=True), (nb, LANES))

    part[...] = jnp.zeros((8, YZ), F32)
    base[...] = jnp.zeros((8, YZ), F32)
    for x in range(BX):
        loads[x].wait()

        for blk in range(YZ // LANES):
            cols = slice(LANES * blk, LANES * (blk + 1))
            wave = waves[x, :, cols].astype(F32)
            part[x : x + 1, cols] = jnp.sum((wave * occ_col[...]) * wave, 0, keepdims=True)

    def packed(field):
        mean = (jnp.sum(field, 0, keepdims=True) * (1.0 / BX)).astype(BF16).astype(F32)
        row = iota(field.shape, 0)
        return jnp.where(row < BX, field - mean, jnp.where(row == BX, mean, 0.0)).astype(BF16)

    def unpacked(block):
        return block + block[BX : BX + 1]

    gath[band] = packed(part[...])

    one = lambda flag: jnp.where(flag, 1, 0)
    n_dom = (1 + one(has_xlo) + one(has_xhi)) * (1 + one(has_ylo) + one(has_yhi)) * 2 - 1
    pl.semaphore_wait(barrier, n_dom + n_band - 1)
    band_in = [
        send(
            remote(gath.at[band], gath.at[band], BAND + d, BAND + d, {"dom": me, "band": (band + d) % n_band}),
            None, None,
        )
        for d in range(1, n_band)
    ]

    cp_prev.wait()
    cp_comp.wait()
    cp_loc.wait()
    send_v[...] = pvx[EDGE : EDGE + OWN, :].astype(BF16)
    send_c[...] = cmx[EDGE : EDGE + OWN, :].astype(BF16)
    px_in = []
    for n, (src, dst) in enumerate(((send_v, edge_v), (send_c, edge_c))):
        px_in.append(send(
            remote(src.at[pl.ds(0, EDGE)], dst.at[0], POT_X + 2 * n, POT_X + 2 * n, neighbour(-1, 0, 0)),
            has_xlo, has_xhi,
        ))
        px_in.append(send(
            remote(
                src.at[pl.ds(OWN - EDGE, EDGE)], dst.at[1], POT_X + 2 * n + 1, POT_X + 2 * n + 1, neighbour(1, 0, 0)
            ),
            has_xhi, has_xlo,
        ))

    orb_in = [
        send(remote(orb.at[0], xhi, ORB_X, ORB_X, neighbour(-1, 0, 0)), has_xlo, has_xhi),
        send(remote(orb.at[BX - 1], xlo, ORB_X + 1, ORB_X + 1, neighbour(1, 0, 0)), has_xhi, has_xlo),
        send(
            remote(orb.at[:, :, pl.ds(0, LANES)], yhi, ORB_Y, ORB_Y, neighbour(0, -1, 0)), has_ylo, has_yhi
        ),
        send(
            remote(orb.at[:, :, pl.ds(YZ - LANES, LANES)], ylo, ORB_Y + 1, ORB_Y + 1, neighbour(0, 1, 0)),
            has_yhi, has_ylo,
        ),
        send(remote(orb, zbuf, ORB_Z, ORB_Z, neighbour(0, 0, 1)), None, None),
    ]

    def zero(ref, *index):
        def run():
            view = ref.at[index] if index else ref
            view[...] = jnp.zeros(view.shape, view.dtype)
        return run

    when(jnp.logical_not(has_xhi), zero(xhi))
    when(jnp.logical_not(has_xlo), zero(xlo))
    for ref in (edge_v, edge_c):
        when(jnp.logical_not(has_xhi), zero(ref, 0))
        when(jnp.logical_not(has_xlo), zero(ref, 1))
    when(jnp.logical_not(has_ylo), zero(ylo))
    when(jnp.logical_not(has_yhi), zero(yhi))
    for dx, dy, dz in OFFSETS:
        cond = exists(dx, dy)
        if cond is not None:
            when(jnp.logical_not(cond), zero(rh, slot_of(dx, dy, dz)))
    when(jnp.logical_not(has_yhi), zero(rim_in, 0))
    when(jnp.logical_not(has_ylo), zero(rim_in, 1))
    for x in range(NX):
        for ref in (va, vb):
            ref[x, 0:8, :] = jnp.zeros((8, LANES), F32)
            ref[x, Y0 + FY + 8 :, :] = jnp.zeros((8, LANES), F32)
    cbuf[...] = jnp.zeros(cbuf.shape, F32)
    xo[...] = jnp.zeros(xo.shape, F32)
    xz[...] = jnp.zeros(xz.shape, F32)

    def fill_w(r, carry):
        row = iota((LANES, 384), 0) + r * LANES
        col = iota((LANES, 384), 1)
        place = iota((1, 384), 1) % BZ
        diff = row - LANES - col
        main = jnp.where(diff == 0, 3.0, 0.0)
        side = (
            (diff == BZ) | (diff == -BZ)
            | ((diff == 1) & (place != BZ - 1)) | ((diff == -1) & (place != 0))
        )
        main = jnp.where(side, -0.5, main)
        far = row - 640 - col
        over = jnp.where(
            bk == 0,
            jnp.where((far == 1 - BZ) & (place == BZ - 1), -0.5, 0.0),
            jnp.where((far == BZ - 1) & (place == 0), -0.5, 0.0),
        )
        w_ref[pl.ds(pl.multiple_of(r * LANES, LANES), LANES), :] = jnp.where(row < 640, main, over).astype(BF16)
        return carry

    lax.fori_loop(0, 8, fill_w, 0)

    arrive(*px_in)
    for full, edge in ((pvx, edge_v), (cmx, edge_c)):
        full[EDGE + OWN : 2 * EDGE + OWN, :] = edge[0].astype(F32)
        full[0:EDGE, :] = edge[1].astype(F32)
    lane12 = iota((12, LANES), 1)

    def split(x):
        base = EDGE - 36 * M + 36 * x
        for n, (src, dst, scale) in enumerate(((pvx, va, None), (cmx, sa, -math.pi))):
            a0, a1, a2 = (src[pl.ds(base + r, 12, stride=3), :] for r in range(3))
            if scale is not None:
                a0, a1, a2 = scale * a0, scale * a1, scale * a2
            cut = lane12 < FZ
            y0 = a0
            y1 = jnp.where(lane12 < 32, pltpu.roll(a0, 32, 1), pltpu.roll(a1, 32, 1))
            y2 = jnp.where(lane12 < 64, pltpu.roll(a1, 64, 1), pltpu.roll(a2, 64, 1))
            y3 = pltpu.roll(a2, 96, 1)
            for q, val in enumerate((y0, y1, y2, y3)):
                dst[x, pl.ds(Y0 + q, 12, stride=4), :] = jnp.where(cut, val, 0.0)
            rim_out[0, n, x] = dst[x, Y0 : Y0 + 8, :].astype(BF16)
            rim_out[1, n, x] = dst[x, Y0 + FY - 8 : Y0 + FY, :].astype(BF16)

    loop(0, NX, split, 2)
    rim_copies = [
        send(remote(rim_out.at[0], rim_in.at[0], POT_Y, POT_Y, neighbour(0, -1, 0)), has_ylo, has_yhi),
        send(remote(rim_out.at[1], rim_in.at[1], POT_Y + 1, POT_Y + 1, neighbour(0, 1, 0)), has_yhi, has_ylo),
    ]

    arrive(*band_in)
    rho = gath[0].astype(F32)
    for d in range(1, n_band):
        rho = rho + gath[d].astype(F32)
    rho = jnp.where(iota((8, YZ), 0) < BX, unpacked(rho), 0.0)
    tot[...] = rho
    totb[...] = packed(rho)
    halo_in = []
    for dx, dy, dz in OFFSETS:
        there = slot_of(-dx, -dy, dz)
        cols = {0: pl.ds(0, YZ), -1: pl.ds(0, 256), 1: pl.ds(YZ - 256, 256)}[dy]
        cp = remote(
            totb.at[:, cols], rh.at[there, :, cols], HALO + slot_of(dx, dy, dz), HALO + there,
            neighbour(dx, dy, dz),
        )
        halo_in.append(send(cp, exists(dx, dy), exists(-dx, -dy)))

    for x in range(BX):
        base[x : x + 1, :] = loc[x]
    base[...] = base[...] - jnp.exp(jnp.log((3.0 / math.pi) * tot[...]) * (1.0 / 3.0))

    arrive(*rim_copies)
    lane = iota((SPAN, LANES), 1)
    span = slice(Y0 - 8, Y0 - 8 + SPAN)
    inner = (lane < M) | ((lane >= 64) & (lane < 64 + M))

    def pack_z(x):
        for n, ref in enumerate((va, sa)):
            ref[x, Y0 + FY : Y0 + FY + 8, :] = rim_in[0, n, x].astype(F32)
            ref[x, Y0 - 8 : Y0, :] = rim_in[1, n, x].astype(F32)
        v, s = va[x, span, :], sa[x, span, :]
        first = jnp.where(lane < 64, v, pltpu.roll(s, 64, 1))
        last = jnp.where(lane < 64, pltpu.roll(v, 16 + M - FZ + LANES, 1), pltpu.roll(s, 80 + M - FZ + LANES, 1))
        zsend[x] = jnp.where(inner, first, last).astype(BF16)

    loop(0, NX, pack_z, 2)
    z_in = send(remote(zsend, zrecv, POT_Z, POT_Z, neighbour(0, 0, 1)), None, None)

    arrive(*orb_in)

    for x in range(BX):
        for t in range(3):
            if t == 0:
                here = [ylo[x], waves[x, :, 0:512]]
            elif t == 1:
                here = [waves[x, :, 256:896]]
            else:
                here = [waves[x, :, 640:1152], yhi[x]]
            cols = slice(384 * t, 384 * (t + 1))
            lhs = jnp.concatenate([*here, zbuf[x, :, cols]], 1)
            out = jnp.dot(lhs, w_ref[...], preferred_element_type=F32)
            below = xlo[:, cols] if x == 0 else waves[x - 1, :, cols]
            above = xhi[:, cols] if x == BX - 1 else waves[x + 1, :, cols]
            stencil[x, :, cols] = out - 0.5 * (below.astype(F32) + above.astype(F32))

    arrive(z_in)
    from_z = jnp.where(bk == 0, jnp.where((lane >= FZ) & (lane < FZ + M), 1, 0), jnp.where(lane >= LANES - M, 1, 0)) == 1
    shift_v = jnp.where(bk == 0, FZ, LANES - M - 16)
    shift_s = jnp.where(bk == 0, FZ - 64, 64 - M - 16)

    def merge(x):
        rim = zrecv[x].astype(F32)
        va[x, span, :] = jnp.where(from_z, pltpu.roll(rim, shift_v, 1), va[x, span, :])
        sa[x, span, :] = jnp.where(from_z, pltpu.roll(rim, shift_s, 1), sa[x, span, :])

    loop(0, NX, merge, 2)

    arrive(*halo_in)
    for dst, dz in ((xo, 0), (xz, 1)):
        for dy, start, width, at in ((0, 0, YZ, 256), (-1, YZ - 256, 256, 0), (1, 0, 256, 256 + YZ)):
            cols = slice(start, start + width)
            own = tot[...] if dz == 0 and dy == 0 else unpacked(rh[slot_of(0, dy, dz), :, cols].astype(F32))
            above = unpacked(rh[slot_of(1, dy, dz), :, cols].astype(F32))
            below = unpacked(rh[slot_of(-1, dy, dz), :, cols].astype(F32))
            lanes = slice(at, at + width)
            dst[0:3, lanes] = below[3:6]
            dst[3:9, lanes] = own[0:6]
            dst[9:12, lanes] = above[0:3]

    def split_rho(g):
        window = pl.ds(pl.multiple_of(g * 384, 384), 512)
        for src, base in ((xo, 0), (xz, 64)):
            block = src[:, window]
            for q in range(8):
                cbuf[g * 8 + q, :, base : base + BZ] = block[:, 112 + BZ * q : 112 + BZ * (q + 1)]

    loop(0, 4, split_rho, 2)
    source_row = iota((LANES, LANES), 0)
    fine_lane = iota((LANES, LANES), 1)
    fine_z = jnp.where(fine_lane >= LANES - M, fine_lane - LANES, fine_lane)
    coarse = jnp.where(source_row < 64, source_row, source_row - 64 + jnp.where(bk == 0, BZ, -BZ))
    real = (source_row < BZ) | ((source_row >= 64) & (source_row < 64 + BZ))
    odd = (fine_z + 128) % 2
    half = (fine_z + 128) // 2 - 64
    wz = jnp.where(coarse == half, 0.75 * math.pi, 0.0)
    wz = jnp.where(coarse == half - 1 + 2 * odd, 0.25 * math.pi, wz)
    wz = jnp.where(real, wz, 0.0)
    fine = jnp.dot(
        cbuf[...].reshape(32 * 16, LANES), wz, precision=EXACT, preferred_element_type=F32
    ).reshape(32, 16, LANES)
    for y in range(30):
        f1[pl.ds(y + 5, 12, stride=40), :] = fine[y, 0:12]

    def refine_y(x):
        base = pl.multiple_of(x * 40, 8)
        block = f1[pl.ds(base, 40), :]
        mid = 0.75 * block[6:34]
        f2[x, pl.ds(4, 28, stride=2), :] = mid + 0.25 * block[5:33]
        f2[x, pl.ds(5, 28, stride=2), :] = mid + 0.25 * block[7:35]

    loop(0, 12, refine_y, 4)

    def refine_x(x):
        mid = 0.75 * f2[x]
        at = 2 * x - 1
        sa[at, span, :] = sa[at, span, :] + mid + 0.25 * f2[x - 1]
        sa[at + 1, span, :] = sa[at + 1, span, :] + mid + 0.25 * f2[x + 1]

    loop(1, 11, refine_x, 5)

    yrow = iota((SPAN, LANES), 0)
    y_ok = ((yrow >= 8) | has_ylo) & ((yrow < 8 + FY) | has_yhi)
    z_ok = (lane < FZ) | from_z
    sixth = jnp.where(y_ok & z_ok, 1.0 / 6.0, 0.0)
    x_low = jnp.where(has_xlo, 1.0, 0.0)
    x_high = jnp.where(has_xhi, 1.0, 0.0)

    for sweep in range(SWEEPS):
        old, new = (va, vb) if sweep % 2 == 0 else (vb, va)

        def update(x, old=old, new=new):
            mid = old[x, span, :]
            acc = old[x - 1, span, :] + old[x + 1, span, :] + sa[x, span, :]
            acc = acc + (old[x, Y0 - 9 : Y0 - 9 + SPAN, :] + old[x, Y0 - 7 : Y0 - 7 + SPAN, :])
            acc = acc + pltpu.roll(mid, 1, 1) + pltpu.roll(mid, LANES - 1, 1)
            factor = jnp.where(x < M, x_low, jnp.where(x >= M + FX, x_high, 1.0))
            new[x, span, :] = acc * (sixth * factor)

        loop(1 + sweep, NX - 1 - sweep, update, (5, 6, 4, 7)[sweep])

    for x in range(BX):
        at = 2 * x + M
        g3[x, 0:YROWS, :] = 0.125 * (va[at - 1] + va[at + 2]) + 0.375 * (va[at] + va[at + 1])
    for x in range(BX):
        c3[BY * x : BY * (x + 1), :] = 0.125 * (
            g3[x, pl.ds(Y0 - 1, BY, stride=2), :] + g3[x, pl.ds(Y0 + 2, BY, stride=2), :]
        ) + 0.375 * (g3[x, pl.ds(Y0, BY, stride=2), :] + g3[x, pl.ds(Y0 + 1, BY, stride=2), :])
    lane_in = iota((LANES, LANES), 0)
    cell = iota((LANES, LANES), 1)
    rel = jnp.where(lane_in == LANES - 1, -1, lane_in) - 2 * cell
    wr = jnp.where((rel == 0) | (rel == 1), 0.375, 0.0)
    wr = jnp.where((rel == -1) | (rel == 2), 0.125, wr)
    wr = jnp.where(cell < BZ, wr, 0.0)
    c3[...] = jnp.dot(c3[...], wr, precision=EXACT, preferred_element_type=F32)
    for y in range(BY):
        tmp_m[0:BX, y * BZ : (y + 1) * BZ] = c3[pl.ds(y, BX, stride=BY), :][:, 0:BZ]
    eff_out[...] = tmp_m[0:BX, :] + base[0:BX, :]

    def join(x):
        p0, p1, p2, p3 = (va[x + M, pl.ds(Y0 + q, 12, stride=4), :] for q in range(4))
        r0 = jnp.where(lane12 < 96, p0, pltpu.roll(p1, 96, 1))
        r1 = jnp.where(lane12 < 64, pltpu.roll(p1, 96, 1), pltpu.roll(p2, 64, 1))
        r2 = jnp.where(lane12 < 32, pltpu.roll(p2, 64, 1), pltpu.roll(p3, 32, 1))
        for r, val in enumerate((r0, r1, r2)):
            pot_out[pl.ds(36 * x + r, 12, stride=3), :] = val

    loop(0, FX, join, 6)

    finish()


def solution(mesh):
    n_band = mesh.shape["band"]
    domains = mesh.shape["dom"]
    ny = min(4, domains // 4)
    nx = domains // (ny * 2)

    def local(orbitals, occupations, previous, compensation, local_potential):
        nb = orbitals.shape[0]
        hbm = pl.BlockSpec(memory_space=pltpu.HBM)
        vmem = pl.BlockSpec(memory_space=pltpu.VMEM)
        waves = orbitals[:, 0].transpose(1, 0, 2)
        stencil, effective, potential, held = pl.pallas_call(
            functools.partial(step_kernel, (nb, n_band, nx, ny)),
            out_shape=(
                jax.ShapeDtypeStruct((BX, nb, YZ), F32),
                jax.ShapeDtypeStruct((BX, YZ), F32),
                jax.ShapeDtypeStruct((OWN, LANES), F32),
                jax.ShapeDtypeStruct((BX, nb, YZ), BF16),
            ),
            in_specs=[hbm] * 5,
            out_specs=(vmem,) * 4,
            scratch_shapes=[
                pltpu.VMEM((nb, YZ), BF16),
                pltpu.VMEM((nb, YZ), BF16),
                pltpu.VMEM((BX, nb, YZ), BF16),
                pltpu.VMEM((BX, nb, LANES), BF16),
                pltpu.VMEM((BX, nb, LANES), BF16),
                pltpu.VMEM((1024, 384), BF16),
                pltpu.VMEM((1, nb), F32),
                pltpu.VMEM((nb, LANES), F32),
                pltpu.VMEM((2 * EDGE + OWN, LANES), F32),
                pltpu.VMEM((2 * EDGE + OWN, LANES), F32),
                pltpu.VMEM((OWN, LANES), BF16),
                pltpu.VMEM((OWN, LANES), BF16),
                pltpu.VMEM((2, EDGE, LANES), BF16),
                pltpu.VMEM((2, EDGE, LANES), BF16),
                pltpu.VMEM((BX, 1, YZ), F32),
            ]
            + [pltpu.VMEM((NX, YROWS, LANES), F32)] * 3
            + [
                pltpu.VMEM((2, 2, NX, 8, LANES), BF16),
                pltpu.VMEM((2, 2, NX, 8, LANES), BF16),
                pltpu.VMEM((NX, SPAN, LANES), BF16),
                pltpu.VMEM((NX, SPAN, LANES), BF16),
                pltpu.VMEM((8, YZ), F32),
                pltpu.VMEM((n_band, 8, YZ), BF16),
                pltpu.VMEM((8, YZ), F32),
                pltpu.VMEM((8, YZ), BF16),
                pltpu.VMEM((18, 8, YZ), BF16),
                pltpu.VMEM((16, 512 + YZ), F32),
                pltpu.VMEM((16, 512 + YZ), F32),
                pltpu.VMEM((32, 16, LANES), F32),
                pltpu.VMEM((12 * 40, LANES), F32),
                pltpu.VMEM((12, SPAN, LANES), F32),
                pltpu.VMEM((BX, YROWS, LANES), F32),
                pltpu.VMEM((BX * BY, LANES), F32),
                pltpu.VMEM((8, YZ), F32),
                pltpu.VMEM((8, YZ), F32),
                pltpu.SemaphoreType.DMA((BX + 4,)),
                pltpu.SemaphoreType.DMA((N_SEM,)),
                pltpu.SemaphoreType.DMA((N_SEM,)),
            ],
            compiler_params=pltpu.CompilerParams(
                collective_id=0, has_side_effects=True, vmem_limit_bytes=48 * 1024 * 1024
            ),
        )(
            pltpu.with_memory_space_constraint(waves, pltpu.HBM),
            pltpu.with_memory_space_constraint(occupations.reshape(1, nb), pltpu.HBM),
            pltpu.with_memory_space_constraint(previous.reshape(OWN, LANES), pltpu.HBM),
            pltpu.with_memory_space_constraint(compensation.reshape(OWN, LANES), pltpu.HBM),
            pltpu.with_memory_space_constraint(local_potential.reshape(BX, 1, YZ), pltpu.HBM),
        )
        applied = (stencil + effective[:, None] * held.astype(F32)).astype(BF16)
        return applied.transpose(1, 0, 2)[:, None], potential.reshape(previous.shape)

    return jax.shard_map(
        local,
        mesh=mesh,
        in_specs=(
            P("band", "dom", None, None),
            P("band"),
            P("dom", None, None),
            P("dom", None, None),
            P("dom", None, None),
        ),
        out_specs=(P("band", "dom", None, None), P("dom", None, None)),
        check_vma=False,
    )
```

```python
import functools
import math

import jax
import jax.numpy as jnp
from jax import lax
from jax.experimental import pallas as pl
from jax.experimental.pallas import tpu as pltpu
from jax.sharding import PartitionSpec as P

BX, BY, BZ = 6, 24, 48
YZ = BY * BZ
FX, FY, FZ = 2 * BX, 2 * BY, 2 * BZ
FYZ = FY * FZ
BANDS = 768
SWEEPS = 4
M = 5
NX = FX + 2 * M
Y0 = 16
YROWS = FY + 2 * Y0
SPAN = FY + 16
EDGE = 192
OWN = FX * 36
LANES = 128
MESH = pl.DeviceIdType.MESH
F32, BF16 = jnp.float32, jnp.bfloat16
EXACT = lax.Precision.HIGHEST

OFFSETS = [
    (dx, dy, dz) for dx in (-1, 0, 1) for dy in (-1, 0, 1) for dz in (0, 1) if (dx, dy, dz) != (0, 0, 0)
]


def slot_of(dx, dy, dz):
    return ((dx + 1) * 3 + dy + 1) * 2 + dz


HALO = 0
BAND = 18
ORB_X, ORB_Y, ORB_Z = 26, 30, 32
POT_X, POT_Y, POT_Z = 33, 37, 43
N_SEM = 44


def loop(low, high, body, together):
    def some(step, carry):
        for u in range(together):
            body(low + step * together + u)
        return carry

    assert (high - low) % together == 0
    lax.fori_loop(0, (high - low) // together, some, 0)


def iota(shape, axis):
    return lax.broadcasted_iota(jnp.int32, shape, axis)


def step_kernel(
    sizes,
    orb, occ_in, prev_in, comp_in, loc_in,
    stencil, eff_out, pot_out, waves,
    xlo, xhi, zbuf, ylo, yhi, w_ref, occ, occ_col,
    pvx, cmx, send_v, send_c, edge_v, edge_c, loc,
    va, vb, sa, rim_tmp, rim_out, rim_in, rim_all, zsend, zrecv,
    part, gath, tot, totb, rh, xo, xz, cbuf, f1, f2, g3, c3, tmp_m, base,
    load_sem, send_sem, recv_sem,
):
    nb, n_band, nx, ny = sizes
    me = lax.axis_index("dom")
    band = lax.axis_index("band")
    bi = me // (ny * 2)
    bj = (me // 2) % ny
    bk = me % 2
    has_xlo, has_xhi = bi > 0, bi < nx - 1
    has_ylo, has_yhi = bj > 0, bj < ny - 1

    def exists(dx, dy):
        ok = None
        for flag in ([has_xlo] if dx < 0 else [has_xhi] if dx > 0 else []) + (
            [has_ylo] if dy < 0 else [has_yhi] if dy > 0 else []
        ):
            ok = flag if ok is None else jnp.logical_and(ok, flag)
        return ok

    def when(cond, fn):
        if cond is None:
            fn()
        else:
            pl.when(cond)(fn)

    def neighbour(dx, dy, dz):
        other = (1 - bk) if dz else bk
        return {"dom": ((bi + dx) * ny + bj + dy) * 2 + other, "band": band}

    def remote(src, dst, s_idx, r_idx, device):
        return pltpu.make_async_remote_copy(
            src_ref=src, dst_ref=dst, send_sem=send_sem.at[s_idx], recv_sem=recv_sem.at[r_idx],
            device_id=device, device_id_type=MESH,
        )

    leftovers = []

    def send(cp, where, arrival):
        when(where, cp.start)
        handle = [cp, arrival, False]
        leftovers.append((handle, where))
        return handle

    def arrive(*handles):
        for handle in handles:
            when(handle[1], handle[0].wait_recv)
            handle[2] = True

    def finish():
        for handle, where in leftovers:
            if not handle[2]:
                arrive(handle)
            when(where, handle[0].wait_send)

    cp_occ = pltpu.make_async_copy(occ_in, occ, load_sem.at[BX])
    cp_prev = pltpu.make_async_copy(prev_in, pvx.at[pl.ds(EDGE, OWN)], load_sem.at[BX + 1])
    cp_comp = pltpu.make_async_copy(comp_in, cmx.at[pl.ds(EDGE, OWN)], load_sem.at[BX + 2])
    cp_loc = pltpu.make_async_copy(loc_in, loc, load_sem.at[BX + 3])
    loads = [pltpu.make_async_copy(orb.at[x], waves.at[x], load_sem.at[x]) for x in range(BX)]
    cp_occ.start()
    for cp in loads:
        cp.start()
    cp_prev.start()
    cp_comp.start()
    cp_loc.start()

    barrier = pltpu.get_barrier_semaphore()
    for d in range(1, n_band):
        pl.semaphore_signal(
            barrier, inc=1, device_id={"dom": me, "band": (band + d) % n_band}, device_id_type=MESH
        )
    for dx, dy, dz in OFFSETS:
        def greet(dx=dx, dy=dy, dz=dz):
            pl.semaphore_signal(barrier, inc=1, device_id=neighbour(dx, dy, dz), device_id_type=MESH)
        when(exists(dx, dy), greet)

    cp_occ.wait()
    diagonal = jnp.where(iota((nb, nb), 0) == iota((nb, nb), 1), occ[...] * (1.0 / BANDS), 0.0)
    occ_col[...] = jnp.broadcast_to(jnp.sum(diagonal, 1, keepdims=True), (nb, LANES))

    part[...] = jnp.zeros((8, YZ), F32)
    base[...] = jnp.zeros((8, YZ), F32)
    for x in range(BX):
        loads[x].wait()

        for blk in range(YZ // LANES):
            cols = slice(LANES * blk, LANES * (blk + 1))
            wave = waves[x, :, cols].astype(F32)
            part[x : x + 1, cols] = jnp.sum((wave * occ_col[...]) * wave, 0, keepdims=True)

    def packed(field):
        mean = (jnp.sum(field, 0, keepdims=True) * (1.0 / BX)).astype(BF16).astype(F32)
        row = iota(field.shape, 0)
        return jnp.where(row < BX, field - mean, jnp.where(row == BX, mean, 0.0)).astype(BF16)

    def unpacked(block):
        return block + block[BX : BX + 1]

    gath[band] = packed(part[...])

    one = lambda flag: jnp.where(flag, 1, 0)
    n_dom = (1 + one(has_xlo) + one(has_xhi)) * (1 + one(has_ylo) + one(has_yhi)) * 2 - 1
    pl.semaphore_wait(barrier, n_dom + n_band - 1)
    band_in = [
        send(
            remote(gath.at[band], gath.at[band], BAND + d, BAND + d, {"dom": me, "band": (band + d) % n_band}),
            None, None,
        )
        for d in range(1, n_band)
    ]

    cp_prev.wait()
    cp_comp.wait()
    cp_loc.wait()
    send_v[...] = pvx[EDGE : EDGE + OWN, :].astype(BF16)
    send_c[...] = cmx[EDGE : EDGE + OWN, :].astype(BF16)
    px_in = []
    for n, (src, dst) in enumerate(((send_v, edge_v), (send_c, edge_c))):
        px_in.append(send(
            remote(src.at[pl.ds(0, EDGE)], dst.at[0], POT_X + 2 * n, POT_X + 2 * n, neighbour(-1, 0, 0)),
            has_xlo, has_xhi,
        ))
        px_in.append(send(
            remote(
                src.at[pl.ds(OWN - EDGE, EDGE)], dst.at[1], POT_X + 2 * n + 1, POT_X + 2 * n + 1, neighbour(1, 0, 0)
            ),
            has_xhi, has_xlo,
        ))

    for x in range(FX):
        for n, src in enumerate((pvx, cmx)):
            at = EDGE + 36 * x
            rim_tmp[0, n, 4 * x : 4 * x + 4, :] = src[at : at + 4, :]
            rim_tmp[1, n, 4 * x : 4 * x + 4, :] = src[at + 32 : at + 36, :]
    rim_out[...] = rim_tmp[...].astype(BF16)
    rim_copies = []
    for side, dy in ((0, -1), (1, 1)):
        for dx in (0, -1, 1):
            rows = {0: pl.ds(0, 48), -1: pl.ds(0, 32), 1: pl.ds(16, 32)}[dx]
            cp = remote(
                rim_out.at[side, :, rows], rim_in.at[1 - dx, side, :, rows],
                POT_Y + 3 * side + dx + 1, POT_Y + 3 * side + dx + 1, neighbour(dx, dy, 0),
            )
            rim_copies.append(send(cp, exists(dx, dy), exists(-dx, -dy)))

    half = pl.ds(0, nb // 2), pl.ds(nb // 2, nb // 2)

    def orbitals_along_x(n):
        return [
            send(
                remote(orb.at[0, half[n]], xhi.at[half[n]], ORB_X + 2 * n, ORB_X + 2 * n, neighbour(-1, 0, 0)),
                has_xlo, has_xhi,
            ),
            send(
                remote(
                    orb.at[BX - 1, half[n]], xlo.at[half[n]], ORB_X + 2 * n + 1, ORB_X + 2 * n + 1, neighbour(1, 0, 0)
                ),
                has_xhi, has_xlo,
            ),
        ]

    orb_in = [
        send(
            remote(orb.at[:, :, pl.ds(0, LANES)], yhi, ORB_Y, ORB_Y, neighbour(0, -1, 0)), has_ylo, has_yhi
        ),
        send(
            remote(orb.at[:, :, pl.ds(YZ - LANES, LANES)], ylo, ORB_Y + 1, ORB_Y + 1, neighbour(0, 1, 0)),
            has_yhi, has_ylo,
        ),
        send(remote(orb, zbuf, ORB_Z, ORB_Z, neighbour(0, 0, 1)), None, None),
    ]
    orb_x_in = orbitals_along_x(0)

    def zero(ref, *index):
        def run():
            view = ref.at[index] if index else ref
            view[...] = jnp.zeros(view.shape, view.dtype)
        return run

    when(jnp.logical_not(has_xhi), zero(xhi))
    when(jnp.logical_not(has_xlo), zero(xlo))
    for ref in (edge_v, edge_c):
        when(jnp.logical_not(has_xhi), zero(ref, 0))
        when(jnp.logical_not(has_xlo), zero(ref, 1))
    when(jnp.logical_not(has_ylo), zero(ylo))
    when(jnp.logical_not(has_yhi), zero(yhi))
    for dx, dy, dz in OFFSETS:
        cond = exists(dx, dy)
        if cond is not None:
            when(jnp.logical_not(cond), zero(rh, slot_of(dx, dy, dz)))
    for side, dy in ((0, -1), (1, 1)):
        for dx in (-1, 0, 1):
            when(jnp.logical_not(exists(-dx, -dy)), zero(rim_in, 1 - dx, side))
    for x in range(NX):
        for ref in (va, vb, sa):
            ref[x, 0:Y0, :] = jnp.zeros((Y0, LANES), F32)
            ref[x, Y0 + FY :, :] = jnp.zeros((Y0, LANES), F32)
    cbuf[...] = jnp.zeros(cbuf.shape, F32)
    xo[...] = jnp.zeros(xo.shape, F32)
    xz[...] = jnp.zeros(xz.shape, F32)

    def fill_w(r, carry):
        row = iota((LANES, 384), 0) + r * LANES
        col = iota((LANES, 384), 1)
        place = iota((1, 384), 1) % BZ
        diff = row - LANES - col
        main = jnp.where(diff == 0, 3.0, 0.0)
        side = (
            (diff == BZ) | (diff == -BZ)
            | ((diff == 1) & (place != BZ - 1)) | ((diff == -1) & (place != 0))
        )
        main = jnp.where(side, -0.5, main)
        far = row - 640 - col
        over = jnp.where(
            bk == 0,
            jnp.where((far == 1 - BZ) & (place == BZ - 1), -0.5, 0.0),
            jnp.where((far == BZ - 1) & (place == 0), -0.5, 0.0),
        )
        w_ref[pl.ds(pl.multiple_of(r * LANES, LANES), LANES), :] = jnp.where(row < 640, main, over).astype(BF16)
        return carry

    lax.fori_loop(0, 8, fill_w, 0)

    lane12 = iota((12, LANES), 1)

    def thread(a0, a1, a2, lanes):
        y0 = a0
        y1 = jnp.where(lanes < 32, pltpu.roll(a0, 32, 1), pltpu.roll(a1, 32, 1))
        y2 = jnp.where(lanes < 64, pltpu.roll(a1, 64, 1), pltpu.roll(a2, 64, 1))
        y3 = pltpu.roll(a2, 96, 1)
        return [jnp.where(lanes < FZ, val, 0.0) for val in (y0, y1, y2, y3)]

    fields = ((pvx, va, 1.0), (cmx, sa, -math.pi))

    def split(x):
        base = EDGE - 36 * M + 36 * x
        for src, dst, scale in fields:
            rows = [scale * src[pl.ds(base + r, 12, stride=3), :] for r in range(3)]
            for q, val in enumerate(thread(*rows, lane12)):
                dst[x, pl.ds(Y0 + q, 12, stride=4), :] = val

    loop(M, M + FX, split, 6)

    arrive(*band_in)
    rho = gath[0].astype(F32)
    for d in range(1, n_band):
        rho = rho + gath[d].astype(F32)
    rho = jnp.where(iota((8, YZ), 0) < BX, unpacked(rho), 0.0)
    tot[...] = rho
    totb[...] = packed(rho)
    halo_in = []
    for dx, dy, dz in OFFSETS:
        there = slot_of(-dx, -dy, dz)
        cols = {0: pl.ds(0, YZ), -1: pl.ds(0, 256), 1: pl.ds(YZ - 256, 256)}[dy]
        cp = remote(
            totb.at[:, cols], rh.at[there, :, cols], HALO + slot_of(dx, dy, dz), HALO + there,
            neighbour(dx, dy, dz),
        )
        halo_in.append(send(cp, exists(dx, dy), exists(-dx, -dy)))

    orb_x_in = orb_x_in + orbitals_along_x(1)

    arrive(*px_in)
    for full, edge in ((pvx, edge_v), (cmx, edge_c)):
        full[EDGE + OWN : 2 * EDGE + OWN, :] = edge[0].astype(F32)
        full[0:EDGE, :] = edge[1].astype(F32)
    loop(0, M, split, 5)
    loop(M + FX, NX, split, 5)
    arrive(*rim_copies)
    lane22 = iota((NX, LANES), 1)
    for n, (_, dst, scale) in enumerate(fields):
        flat = dst.reshape(NX * YROWS, LANES)
        for side in range(2):
            rim_tmp[0, 0, 0:20, :] = rim_in[0, side, n].astype(F32)[28:48]
            rim_tmp[0, 0, 20:48, :] = rim_in[1, side, n].astype(F32)[0:28]
            rim_tmp[0, 1, 0:20, :] = rim_in[1, side, n].astype(F32)[28:48]
            rim_tmp[0, 1, 20:40, :] = rim_in[2, side, n].astype(F32)[0:20]
            rim_all[side, n, 0:48, :] = rim_tmp[0, 0]
            rim_all[side, n, 48:88, :] = rim_tmp[0, 1, 0:40, :]
            a = [scale * rim_all[side, n, pl.ds(r, NX, stride=4), :] for r in range(4)]
            if side == 0:
                cells = [*thread(a[0], a[1], a[2], lane22), jnp.where(lane22 < FZ, a[3], 0.0)]
                first = Y0 + FY
            else:
                cells = [jnp.where(lane22 < FZ, pltpu.roll(a[0], 96, 1), 0.0), *thread(a[1], a[2], a[3], lane22)]
                first = Y0 - M
            for q, val in enumerate(cells):
                flat[pl.ds(first + q, NX, stride=YROWS), :] = val

    lane = iota((SPAN, LANES), 1)
    span = slice(Y0 - 8, Y0 - 8 + SPAN)
    inner = (lane < M) | ((lane >= 64) & (lane < 64 + M))

    def pack_z(x):
        v, s = va[x, span, :], sa[x, span, :]
        first = jnp.where(lane < 64, v, pltpu.roll(s, 64, 1))
        last = jnp.where(lane < 64, pltpu.roll(v, 16 + M - FZ + LANES, 1), pltpu.roll(s, 80 + M - FZ + LANES, 1))
        zsend[x] = jnp.where(inner, first, last).astype(BF16)

    loop(0, NX, pack_z, 2)
    z_in = send(remote(zsend, zrecv, POT_Z, POT_Z, neighbour(0, 0, 1)), None, None)

    for x in range(BX):
        base[x : x + 1, :] = loc[x]
    base[...] = base[...] - jnp.exp(jnp.log((3.0 / math.pi) * tot[...]) * (1.0 / 3.0))

    def stencil_of(x):
        for t in range(3):
            if t == 0:
                here = [ylo[x], waves[x, :, 0:512]]
            elif t == 1:
                here = [waves[x, :, 256:896]]
            else:
                here = [waves[x, :, 640:1152], yhi[x]]
            cols = slice(384 * t, 384 * (t + 1))
            lhs = jnp.concatenate([*here, zbuf[x, :, cols]], 1)
            out = jnp.dot(lhs, w_ref[...], preferred_element_type=F32)
            below = xlo[:, cols] if x == 0 else waves[x - 1, :, cols]
            above = xhi[:, cols] if x == BX - 1 else waves[x + 1, :, cols]
            stencil[x, :, cols] = out - 0.5 * (below.astype(F32) + above.astype(F32))

    arrive(*orb_in)
    for x in range(1, BX - 1):
        stencil_of(x)

    arrive(z_in)
    from_z = jnp.where(bk == 0, jnp.where((lane >= FZ) & (lane < FZ + M), 1, 0), jnp.where(lane >= LANES - M, 1, 0)) == 1
    shift_v = jnp.where(bk == 0, FZ, LANES - M - 16)
    shift_s = jnp.where(bk == 0, FZ - 64, 64 - M - 16)

    def merge(x):
        rim = zrecv[x].astype(F32)
        va[x, span, :] = jnp.where(from_z, pltpu.roll(rim, shift_v, 1), va[x, span, :])
        sa[x, span, :] = jnp.where(from_z, pltpu.roll(rim, shift_s, 1), sa[x, span, :])

    loop(0, NX, merge, 2)

    arrive(*orb_x_in)
    stencil_of(0)
    stencil_of(BX - 1)

    arrive(*halo_in)
    for dst, dz in ((xo, 0), (xz, 1)):
        for dy, start, width, at in ((0, 0, YZ, 256), (-1, YZ - 256, 256, 0), (1, 0, 256, 256 + YZ)):
            cols = slice(start, start + width)
            own = tot[...] if dz == 0 and dy == 0 else unpacked(rh[slot_of(0, dy, dz), :, cols].astype(F32))
            above = unpacked(rh[slot_of(1, dy, dz), :, cols].astype(F32))
            below = unpacked(rh[slot_of(-1, dy, dz), :, cols].astype(F32))
            lanes = slice(at, at + width)
            dst[0:3, lanes] = below[3:6]
            dst[3:9, lanes] = own[0:6]
            dst[9:12, lanes] = above[0:3]

    def split_rho(g):
        window = pl.ds(pl.multiple_of(g * 384, 384), 512)
        for src, base in ((xo, 0), (xz, 64)):
            block = src[:, window]
            for q in range(8):
                cbuf[g * 8 + q, :, base : base + BZ] = block[:, 112 + BZ * q : 112 + BZ * (q + 1)]

    loop(0, 4, split_rho, 2)
    source_row = iota((LANES, LANES), 0)
    fine_lane = iota((LANES, LANES), 1)
    fine_z = jnp.where(fine_lane >= LANES - M, fine_lane - LANES, fine_lane)
    coarse = jnp.where(source_row < 64, source_row, source_row - 64 + jnp.where(bk == 0, BZ, -BZ))
    real = (source_row < BZ) | ((source_row >= 64) & (source_row < 64 + BZ))
    odd = (fine_z + 128) % 2
    floor = (fine_z + 128) // 2 - 64
    wz = jnp.where(coarse == floor, 0.75 * math.pi, 0.0)
    wz = jnp.where(coarse == floor - 1 + 2 * odd, 0.25 * math.pi, wz)
    wz = jnp.where(real, wz, 0.0)
    fine = jnp.dot(
        cbuf[...].reshape(32 * 16, LANES), wz, precision=EXACT, preferred_element_type=F32
    ).reshape(32, 16, LANES)
    for y in range(30):
        f1[pl.ds(y + 5, 12, stride=40), :] = fine[y, 0:12]

    def refine_y(x):
        base = pl.multiple_of(x * 40, 8)
        block = f1[pl.ds(base, 40), :]
        mid = 0.75 * block[6:34]
        f2[x, pl.ds(4, 28, stride=2), :] = mid + 0.25 * block[5:33]
        f2[x, pl.ds(5, 28, stride=2), :] = mid + 0.25 * block[7:35]

    loop(0, 12, refine_y, 4)

    def refine_x(x):
        mid = 0.75 * f2[x]
        at = 2 * x - 1
        sa[at, span, :] = sa[at, span, :] + mid + 0.25 * f2[x - 1]
        sa[at + 1, span, :] = sa[at + 1, span, :] + mid + 0.25 * f2[x + 1]

    loop(1, 11, refine_x, 5)

    yrow = iota((SPAN, LANES), 0)
    y_ok = ((yrow >= 8) | has_ylo) & ((yrow < 8 + FY) | has_yhi)
    z_ok = (lane < FZ) | from_z
    sixth = jnp.where(y_ok & z_ok, 1.0 / 6.0, 0.0)
    x_low = jnp.where(has_xlo, 1.0, 0.0)
    x_high = jnp.where(has_xhi, 1.0, 0.0)

    for sweep in range(SWEEPS):
        old, new = (va, vb) if sweep % 2 == 0 else (vb, va)

        def update(x, old=old, new=new):
            mid = old[x, span, :]
            acc = old[x - 1, span, :] + old[x + 1, span, :] + sa[x, span, :]
            acc = acc + (old[x, Y0 - 9 : Y0 - 9 + SPAN, :] + old[x, Y0 - 7 : Y0 - 7 + SPAN, :])
            acc = acc + pltpu.roll(mid, 1, 1) + pltpu.roll(mid, LANES - 1, 1)
            factor = jnp.where(x < M, x_low, jnp.where(x >= M + FX, x_high, 1.0))
            new[x, span, :] = acc * (sixth * factor)

        loop(1 + sweep, NX - 1 - sweep, update, (5, 6, 4, 7)[sweep])

    for x in range(BX):
        at = 2 * x + M
        g3[x, 0:YROWS, :] = 0.125 * (va[at - 1] + va[at + 2]) + 0.375 * (va[at] + va[at + 1])
    for x in range(BX):
        c3[BY * x : BY * (x + 1), :] = 0.125 * (
            g3[x, pl.ds(Y0 - 1, BY, stride=2), :] + g3[x, pl.ds(Y0 + 2, BY, stride=2), :]
        ) + 0.375 * (g3[x, pl.ds(Y0, BY, stride=2), :] + g3[x, pl.ds(Y0 + 1, BY, stride=2), :])
    lane_in = iota((LANES, LANES), 0)
    cell = iota((LANES, LANES), 1)
    rel = jnp.where(lane_in == LANES - 1, -1, lane_in) - 2 * cell
    wr = jnp.where((rel == 0) | (rel == 1), 0.375, 0.0)
    wr = jnp.where((rel == -1) | (rel == 2), 0.125, wr)
    wr = jnp.where(cell < BZ, wr, 0.0)
    c3[...] = jnp.dot(c3[...], wr, precision=EXACT, preferred_element_type=F32)
    for y in range(BY):
        tmp_m[0:BX, y * BZ : (y + 1) * BZ] = c3[pl.ds(y, BX, stride=BY), :][:, 0:BZ]
    eff_out[...] = tmp_m[0:BX, :] + base[0:BX, :]

    def join(x):
        p0, p1, p2, p3 = (va[x + M, pl.ds(Y0 + q, 12, stride=4), :] for q in range(4))
        r0 = jnp.where(lane12 < 96, p0, pltpu.roll(p1, 96, 1))
        r1 = jnp.where(lane12 < 64, pltpu.roll(p1, 96, 1), pltpu.roll(p2, 64, 1))
        r2 = jnp.where(lane12 < 32, pltpu.roll(p2, 64, 1), pltpu.roll(p3, 32, 1))
        for r, val in enumerate((r0, r1, r2)):
            pot_out[pl.ds(36 * x + r, 12, stride=3), :] = val

    loop(0, FX, join, 6)

    finish()


def solution(mesh):
    n_band = mesh.shape["band"]
    domains = mesh.shape["dom"]
    ny = min(4, domains // 4)
    nx = domains // (ny * 2)

    def local(orbitals, occupations, previous, compensation, local_potential):
        nb = orbitals.shape[0]
        hbm = pl.BlockSpec(memory_space=pltpu.HBM)
        vmem = pl.BlockSpec(memory_space=pltpu.VMEM)
        waves = orbitals[:, 0].transpose(1, 0, 2)
        stencil, effective, potential, held = pl.pallas_call(
            functools.partial(step_kernel, (nb, n_band, nx, ny)),
            out_shape=(
                jax.ShapeDtypeStruct((BX, nb, YZ), F32),
                jax.ShapeDtypeStruct((BX, YZ), F32),
                jax.ShapeDtypeStruct((OWN, LANES), F32),
                jax.ShapeDtypeStruct((BX, nb, YZ), BF16),
            ),
            in_specs=[hbm] * 5,
            out_specs=(vmem,) * 4,
            scratch_shapes=[
                pltpu.VMEM((nb, YZ), BF16),
                pltpu.VMEM((nb, YZ), BF16),
                pltpu.VMEM((BX, nb, YZ), BF16),
                pltpu.VMEM((BX, nb, LANES), BF16),
                pltpu.VMEM((BX, nb, LANES), BF16),
                pltpu.VMEM((1024, 384), BF16),
                pltpu.VMEM((1, nb), F32),
                pltpu.VMEM((nb, LANES), F32),
                pltpu.VMEM((2 * EDGE + OWN, LANES), F32),
                pltpu.VMEM((2 * EDGE + OWN, LANES), F32),
                pltpu.VMEM((OWN, LANES), BF16),
                pltpu.VMEM((OWN, LANES), BF16),
                pltpu.VMEM((2, EDGE, LANES), BF16),
                pltpu.VMEM((2, EDGE, LANES), BF16),
                pltpu.VMEM((BX, 1, YZ), F32),
            ]
            + [pltpu.VMEM((NX, YROWS, LANES), F32)] * 3
            + [
                pltpu.VMEM((2, 2, 48, LANES), F32),
                pltpu.VMEM((2, 2, 48, LANES), BF16),
                pltpu.VMEM((3, 2, 2, 48, LANES), BF16),
                pltpu.VMEM((2, 2, 88, LANES), F32),
                pltpu.VMEM((NX, SPAN, LANES), BF16),
                pltpu.VMEM((NX, SPAN, LANES), BF16),
                pltpu.VMEM((8, YZ), F32),
                pltpu.VMEM((n_band, 8, YZ), BF16),
                pltpu.VMEM((8, YZ), F32),
                pltpu.VMEM((8, YZ), BF16),
                pltpu.VMEM((18, 8, YZ), BF16),
                pltpu.VMEM((16, 512 + YZ), F32),
                pltpu.VMEM((16, 512 + YZ), F32),
                pltpu.VMEM((32, 16, LANES), F32),
                pltpu.VMEM((12 * 40, LANES), F32),
                pltpu.VMEM((12, SPAN, LANES), F32),
                pltpu.VMEM((BX, YROWS, LANES), F32),
                pltpu.VMEM((BX * BY, LANES), F32),
                pltpu.VMEM((8, YZ), F32),
                pltpu.VMEM((8, YZ), F32),
                pltpu.SemaphoreType.DMA((BX + 4,)),
                pltpu.SemaphoreType.DMA((N_SEM,)),
                pltpu.SemaphoreType.DMA((N_SEM,)),
            ],
            compiler_params=pltpu.CompilerParams(
                collective_id=0, has_side_effects=True, vmem_limit_bytes=48 * 1024 * 1024
            ),
        )(
            pltpu.with_memory_space_constraint(waves, pltpu.HBM),
            pltpu.with_memory_space_constraint(occupations.reshape(1, nb), pltpu.HBM),
            pltpu.with_memory_space_constraint(previous.reshape(OWN, LANES), pltpu.HBM),
            pltpu.with_memory_space_constraint(compensation.reshape(OWN, LANES), pltpu.HBM),
            pltpu.with_memory_space_constraint(local_potential.reshape(BX, 1, YZ), pltpu.HBM),
        )
        applied = (stencil + effective[:, None] * held.astype(F32)).astype(BF16)
        return applied.transpose(1, 0, 2)[:, None], potential.reshape(previous.shape)

    return jax.shard_map(
        local,
        mesh=mesh,
        in_specs=(
            P("band", "dom", None, None),
            P("band"),
            P("dom", None, None),
            P("dom", None, None),
            P("dom", None, None),
        ),
        out_specs=(P("band", "dom", None, None), P("dom", None, None)),
        check_vma=False,
    )
```

```python
import functools
import math

import jax
import jax.numpy as jnp
from jax import lax
from jax.experimental import pallas as pl
from jax.experimental.pallas import tpu as pltpu
from jax.sharding import PartitionSpec as P

BX, BY, BZ = 6, 24, 48
YZ = BY * BZ
FX, FY, FZ = 2 * BX, 2 * BY, 2 * BZ
FYZ = FY * FZ
BANDS = 768
SWEEPS = 4
M = 5
NX = FX + 2 * M
Y0 = 16
YROWS = FY + 2 * Y0
SPAN = FY + 16
EDGE = 192
OWN = FX * 36
LANES = 128
MESH = pl.DeviceIdType.MESH
F32, BF16 = jnp.float32, jnp.bfloat16
EXACT = lax.Precision.HIGHEST

OFFSETS = [
    (dx, dy, dz) for dx in (-1, 0, 1) for dy in (-1, 0, 1) for dz in (0, 1) if (dx, dy, dz) != (0, 0, 0)
]


def slot_of(dx, dy, dz):
    return ((dx + 1) * 3 + dy + 1) * 2 + dz


HALO = 0
BAND = 18
ORB_X, ORB_Y, ORB_Z = 26, 30, 32
POT_X, POT_Y, POT_Z = 33, 37, 43
N_SEM = 44


def loop(low, high, body, together):
    def some(step, carry):
        for u in range(together):
            body(low + step * together + u)
        return carry

    assert (high - low) % together == 0
    lax.fori_loop(0, (high - low) // together, some, 0)


def iota(shape, axis):
    return lax.broadcasted_iota(jnp.int32, shape, axis)


def step_kernel(
    sizes,
    orb, occ_in, prev_in, comp_in, loc_in,
    stencil, eff_out, pot_out, waves,
    xlo, xhi, zbuf, ylo, yhi, w_ref, occ, occ_col,
    pvx, cmx, send_v, send_c, edge_v, edge_c, loc,
    va, vb, sa, rim_tmp, rim_out, rim_in, rim_all, zsend, zrecv,
    part, gath, tot, totb, rh, xo, xz, cbuf, f1, f2, g3, c3, tmp_m, base,
    load_sem, send_sem, recv_sem,
):
    nb, n_band, nx, ny = sizes
    me = lax.axis_index("dom")
    band = lax.axis_index("band")
    bi = me // (ny * 2)
    bj = (me // 2) % ny
    bk = me % 2
    has_xlo, has_xhi = bi > 0, bi < nx - 1
    has_ylo, has_yhi = bj > 0, bj < ny - 1

    def exists(dx, dy):
        ok = None
        for flag in ([has_xlo] if dx < 0 else [has_xhi] if dx > 0 else []) + (
            [has_ylo] if dy < 0 else [has_yhi] if dy > 0 else []
        ):
            ok = flag if ok is None else jnp.logical_and(ok, flag)
        return ok

    def when(cond, fn):
        if cond is None:
            fn()
        else:
            pl.when(cond)(fn)

    def neighbour(dx, dy, dz):
        other = (1 - bk) if dz else bk
        return {"dom": ((bi + dx) * ny + bj + dy) * 2 + other, "band": band}

    def remote(src, dst, s_idx, r_idx, device):
        return pltpu.make_async_remote_copy(
            src_ref=src, dst_ref=dst, send_sem=send_sem.at[s_idx], recv_sem=recv_sem.at[r_idx],
            device_id=device, device_id_type=MESH,
        )

    leftovers = []

    def send(cp, where, arrival):
        when(where, cp.start)
        handle = [cp, arrival, False]
        leftovers.append((handle, where))
        return handle

    def arrive(*handles):
        for handle in handles:
            when(handle[1], handle[0].wait_recv)
            handle[2] = True

    def finish():
        for handle, where in leftovers:
            if not handle[2]:
                arrive(handle)
            when(where, handle[0].wait_send)

    cp_occ = pltpu.make_async_copy(occ_in, occ, load_sem.at[BX])
    cp_prev = pltpu.make_async_copy(prev_in, pvx.at[pl.ds(EDGE, OWN)], load_sem.at[BX + 1])
    cp_comp = pltpu.make_async_copy(comp_in, cmx.at[pl.ds(EDGE, OWN)], load_sem.at[BX + 2])
    cp_loc = pltpu.make_async_copy(loc_in, loc, load_sem.at[BX + 3])
    loads = [pltpu.make_async_copy(orb.at[x], waves.at[x], load_sem.at[x]) for x in range(BX)]
    cp_occ.start()
    for cp in loads:
        cp.start()
    cp_prev.start()
    cp_comp.start()
    cp_loc.start()

    barrier = pltpu.get_barrier_semaphore()
    for d in range(1, n_band):
        pl.semaphore_signal(
            barrier, inc=1, device_id={"dom": me, "band": (band + d) % n_band}, device_id_type=MESH
        )
    for dx, dy, dz in OFFSETS:
        def greet(dx=dx, dy=dy, dz=dz):
            pl.semaphore_signal(barrier, inc=1, device_id=neighbour(dx, dy, dz), device_id_type=MESH)
        when(exists(dx, dy), greet)

    cp_occ.wait()
    diagonal = jnp.where(iota((nb, nb), 0) == iota((nb, nb), 1), occ[...] * (1.0 / BANDS), 0.0)
    occ_col[...] = jnp.broadcast_to(jnp.sum(diagonal, 1, keepdims=True), (nb, LANES))

    part[...] = jnp.zeros((8, YZ), F32)
    base[...] = jnp.zeros((8, YZ), F32)
    for x in range(BX):
        loads[x].wait()

        for blk in range(YZ // LANES):
            cols = slice(LANES * blk, LANES * (blk + 1))
            wave = waves[x, :, cols].astype(F32)
            part[x : x + 1, cols] = jnp.sum((wave * occ_col[...]) * wave, 0, keepdims=True)

    def packed(field):
        mean = (jnp.sum(field, 0, keepdims=True) * (1.0 / BX)).astype(BF16).astype(F32)
        row = iota(field.shape, 0)
        return jnp.where(row < BX, field - mean, jnp.where(row == BX, mean, 0.0)).astype(BF16)

    def unpacked(block):
        return block + block[BX : BX + 1]

    gath[band] = packed(part[...])

    one = lambda flag: jnp.where(flag, 1, 0)
    n_dom = (1 + one(has_xlo) + one(has_xhi)) * (1 + one(has_ylo) + one(has_yhi)) * 2 - 1
    pl.semaphore_wait(barrier, n_dom + n_band - 1)
    band_in = [
        send(
            remote(gath.at[band], gath.at[band], BAND + d, BAND + d, {"dom": me, "band": (band + d) % n_band}),
            None, None,
        )
        for d in sorted(range(1, n_band), key=lambda d: -min(d, n_band - d))
    ]

    cp_prev.wait()
    cp_comp.wait()
    cp_loc.wait()
    send_v[...] = pvx[EDGE : EDGE + OWN, :].astype(BF16)
    send_c[...] = cmx[EDGE : EDGE + OWN, :].astype(BF16)
    px_in = []
    for n, (src, dst) in enumerate(((send_v, edge_v), (send_c, edge_c))):
        px_in.append(send(
            remote(src.at[pl.ds(0, EDGE)], dst.at[0], POT_X + 2 * n, POT_X + 2 * n, neighbour(-1, 0, 0)),
            has_xlo, has_xhi,
        ))
        px_in.append(send(
            remote(
                src.at[pl.ds(OWN - EDGE, EDGE)], dst.at[1], POT_X + 2 * n + 1, POT_X + 2 * n + 1, neighbour(1, 0, 0)
            ),
            has_xhi, has_xlo,
        ))

    for x in range(FX):
        for n, src in enumerate((pvx, cmx)):
            at = EDGE + 36 * x
            rim_tmp[0, n, 4 * x : 4 * x + 4, :] = src[at : at + 4, :]
            rim_tmp[1, n, 4 * x : 4 * x + 4, :] = src[at + 32 : at + 36, :]
    rim_out[...] = rim_tmp[...].astype(BF16)
    rim_copies = []
    for side, dy in ((0, -1), (1, 1)):
        for dx in (0, -1, 1):
            rows = {0: pl.ds(0, 48), -1: pl.ds(0, 32), 1: pl.ds(16, 32)}[dx]
            cp = remote(
                rim_out.at[side, :, rows], rim_in.at[1 - dx, side, :, rows],
                POT_Y + 3 * side + dx + 1, POT_Y + 3 * side + dx + 1, neighbour(dx, dy, 0),
            )
            rim_copies.append(send(cp, exists(dx, dy), exists(-dx, -dy)))

    half = pl.ds(0, nb // 2), pl.ds(nb // 2, nb // 2)

    def orbitals_along_x(n):
        return [
            send(
                remote(orb.at[0, half[n]], xhi.at[half[n]], ORB_X + 2 * n, ORB_X + 2 * n, neighbour(-1, 0, 0)),
                has_xlo, has_xhi,
            ),
            send(
                remote(
                    orb.at[BX - 1, half[n]], xlo.at[half[n]], ORB_X + 2 * n + 1, ORB_X + 2 * n + 1, neighbour(1, 0, 0)
                ),
                has_xhi, has_xlo,
            ),
        ]

    orb_in = [
        send(
            remote(orb.at[:, :, pl.ds(0, LANES)], yhi, ORB_Y, ORB_Y, neighbour(0, -1, 0)), has_ylo, has_yhi
        ),
        send(
            remote(orb.at[:, :, pl.ds(YZ - LANES, LANES)], ylo, ORB_Y + 1, ORB_Y + 1, neighbour(0, 1, 0)),
            has_yhi, has_ylo,
        ),
        send(remote(orb, zbuf, ORB_Z, ORB_Z, neighbour(0, 0, 1)), None, None),
    ]
    orb_x_in = orbitals_along_x(0)

    def zero(ref, *index):
        def run():
            view = ref.at[index] if index else ref
            view[...] = jnp.zeros(view.shape, view.dtype)
        return run

    when(jnp.logical_not(has_xhi), zero(xhi))
    when(jnp.logical_not(has_xlo), zero(xlo))
    for ref in (edge_v, edge_c):
        when(jnp.logical_not(has_xhi), zero(ref, 0))
        when(jnp.logical_not(has_xlo), zero(ref, 1))
    when(jnp.logical_not(has_ylo), zero(ylo))
    when(jnp.logical_not(has_yhi), zero(yhi))
    for dx, dy, dz in OFFSETS:
        cond = exists(dx, dy)
        if cond is not None:
            when(jnp.logical_not(cond), zero(rh, slot_of(dx, dy, dz)))
    for side, dy in ((0, -1), (1, 1)):
        for dx in (-1, 0, 1):
            when(jnp.logical_not(exists(-dx, -dy)), zero(rim_in, 1 - dx, side))
    for x in range(NX):
        for ref in (va, vb, sa):
            ref[x, 0:Y0, :] = jnp.zeros((Y0, LANES), F32)
            ref[x, Y0 + FY :, :] = jnp.zeros((Y0, LANES), F32)
    cbuf[...] = jnp.zeros(cbuf.shape, F32)
    xo[...] = jnp.zeros(xo.shape, F32)
    xz[...] = jnp.zeros(xz.shape, F32)

    def fill_w(r, carry):
        row = iota((LANES, 384), 0) + r * LANES
        col = iota((LANES, 384), 1)
        place = iota((1, 384), 1) % BZ
        diff = row - LANES - col
        main = jnp.where(diff == 0, 3.0, 0.0)
        side = (
            (diff == BZ) | (diff == -BZ)
            | ((diff == 1) & (place != BZ - 1)) | ((diff == -1) & (place != 0))
        )
        main = jnp.where(side, -0.5, main)
        far = row - 640 - col
        over = jnp.where(
            bk == 0,
            jnp.where((far == 1 - BZ) & (place == BZ - 1), -0.5, 0.0),
            jnp.where((far == BZ - 1) & (place == 0), -0.5, 0.0),
        )
        w_ref[pl.ds(pl.multiple_of(r * LANES, LANES), LANES), :] = jnp.where(row < 640, main, over).astype(BF16)
        return carry

    lax.fori_loop(0, 8, fill_w, 0)

    lane12 = iota((12, LANES), 1)

    def thread(a0, a1, a2, lanes):
        y0 = a0
        y1 = jnp.where(lanes < 32, pltpu.roll(a0, 32, 1), pltpu.roll(a1, 32, 1))
        y2 = jnp.where(lanes < 64, pltpu.roll(a1, 64, 1), pltpu.roll(a2, 64, 1))
        y3 = pltpu.roll(a2, 96, 1)
        return [jnp.where(lanes < FZ, val, 0.0) for val in (y0, y1, y2, y3)]

    fields = ((pvx, va, 1.0), (cmx, sa, -math.pi))

    def split(x):
        base = EDGE - 36 * M + 36 * x
        for src, dst, scale in fields:
            rows = [scale * src[pl.ds(base + r, 12, stride=3), :] for r in range(3)]
            for q, val in enumerate(thread(*rows, lane12)):
                dst[x, pl.ds(Y0 + q, 12, stride=4), :] = val

    loop(M, M + FX, split, 6)

    arrive(*band_in)
    rho = gath[0].astype(F32)
    for d in range(1, n_band):
        rho = rho + gath[d].astype(F32)
    rho = jnp.where(iota((8, YZ), 0) < BX, unpacked(rho), 0.0)
    tot[...] = rho
    totb[...] = packed(rho)
    halo_in = []
    for dx, dy, dz in sorted(OFFSETS, key=lambda o: (-abs(o[0]) - abs(o[1]), -abs(o[0]), -o[2])):
        there = slot_of(-dx, -dy, dz)
        cols = {0: pl.ds(0, YZ), -1: pl.ds(0, 256), 1: pl.ds(YZ - 256, 256)}[dy]
        cp = remote(
            totb.at[:, cols], rh.at[there, :, cols], HALO + slot_of(dx, dy, dz), HALO + there,
            neighbour(dx, dy, dz),
        )
        halo_in.append(send(cp, exists(dx, dy), exists(-dx, -dy)))

    orb_x_in = orb_x_in + orbitals_along_x(1)

    arrive(*px_in)
    for full, edge in ((pvx, edge_v), (cmx, edge_c)):
        full[EDGE + OWN : 2 * EDGE + OWN, :] = edge[0].astype(F32)
        full[0:EDGE, :] = edge[1].astype(F32)
    loop(0, M, split, 5)
    loop(M + FX, NX, split, 5)
    arrive(*rim_copies)
    lane22 = iota((NX, LANES), 1)
    for n, (_, dst, scale) in enumerate(fields):
        flat = dst.reshape(NX * YROWS, LANES)
        for side in range(2):
            rim_tmp[0, 0, 0:20, :] = rim_in[0, side, n].astype(F32)[28:48]
            rim_tmp[0, 0, 20:48, :] = rim_in[1, side, n].astype(F32)[0:28]
            rim_tmp[0, 1, 0:20, :] = rim_in[1, side, n].astype(F32)[28:48]
            rim_tmp[0, 1, 20:40, :] = rim_in[2, side, n].astype(F32)[0:20]
            rim_all[side, n, 0:48, :] = rim_tmp[0, 0]
            rim_all[side, n, 48:88, :] = rim_tmp[0, 1, 0:40, :]
            a = [scale * rim_all[side, n, pl.ds(r, NX, stride=4), :] for r in range(4)]
            if side == 0:
                cells = [*thread(a[0], a[1], a[2], lane22), jnp.where(lane22 < FZ, a[3], 0.0)]
                first = Y0 + FY
            else:
                cells = [jnp.where(lane22 < FZ, pltpu.roll(a[0], 96, 1), 0.0), *thread(a[1], a[2], a[3], lane22)]
                first = Y0 - M
            for q, val in enumerate(cells):
                flat[pl.ds(first + q, NX, stride=YROWS), :] = val

    lane = iota((SPAN, LANES), 1)
    span = slice(Y0 - 8, Y0 - 8 + SPAN)
    inner = (lane < M) | ((lane >= 64) & (lane < 64 + M))

    def pack_z(x):
        v, s = va[x, span, :], sa[x, span, :]
        first = jnp.where(lane < 64, v, pltpu.roll(s, 64, 1))
        last = jnp.where(lane < 64, pltpu.roll(v, 16 + M - FZ + LANES, 1), pltpu.roll(s, 80 + M - FZ + LANES, 1))
        zsend[x] = jnp.where(inner, first, last).astype(BF16)

    loop(0, NX, pack_z, 11)
    z_in = send(remote(zsend, zrecv, POT_Z, POT_Z, neighbour(0, 0, 1)), None, None)

    for x in range(BX):
        base[x : x + 1, :] = loc[x]
    base[...] = base[...] - jnp.exp(jnp.log((3.0 / math.pi) * tot[...]) * (1.0 / 3.0))

    arrive(*orb_in)
    for first in (0, 3):
        group = slice(first, first + 3)
        for t in range(3):
            if t == 0:
                here = [ylo[group], waves[group, :, 0:512]]
            elif t == 1:
                here = [waves[group, :, 256:896]]
            else:
                here = [waves[group, :, 640:1152], yhi[group]]
            cols = slice(384 * t, 384 * (t + 1))
            lhs = jnp.concatenate([*here, zbuf[group, :, cols]], 2).reshape(3 * nb, 1024)
            out = jnp.dot(lhs, w_ref[...], preferred_element_type=F32).reshape(3, nb, 384)
            for u in range(3):
                x = first + u
                sides = [waves[other, :, cols].astype(F32) for other in (x - 1, x + 1) if 0 <= other < BX]
                stencil[x, :, cols] = out[u] - 0.5 * sum(sides[1:], sides[0])

    arrive(z_in)
    from_z = jnp.where(bk == 0, jnp.where((lane >= FZ) & (lane < FZ + M), 1, 0), jnp.where(lane >= LANES - M, 1, 0)) == 1
    shift_v = jnp.where(bk == 0, FZ, LANES - M - 16)
    shift_s = jnp.where(bk == 0, FZ - 64, 64 - M - 16)

    def merge(x):
        rim = zrecv[x].astype(F32)
        va[x, span, :] = jnp.where(from_z, pltpu.roll(rim, shift_v, 1), va[x, span, :])
        sa[x, span, :] = jnp.where(from_z, pltpu.roll(rim, shift_s, 1), sa[x, span, :])

    loop(0, NX, merge, 11)

    arrive(*orb_x_in)
    stencil[0] = stencil[0] - 0.5 * xlo[...].astype(F32)
    stencil[BX - 1] = stencil[BX - 1] - 0.5 * xhi[...].astype(F32)

    arrive(*halo_in)
    for dst, dz in ((xo, 0), (xz, 1)):
        for dy, start, width, at in ((0, 0, YZ, 256), (-1, YZ - 256, 256, 0), (1, 0, 256, 256 + YZ)):
            cols = slice(start, start + width)
            own = tot[...] if dz == 0 and dy == 0 else unpacked(rh[slot_of(0, dy, dz), :, cols].astype(F32))
            above = unpacked(rh[slot_of(1, dy, dz), :, cols].astype(F32))
            below = unpacked(rh[slot_of(-1, dy, dz), :, cols].astype(F32))
            lanes = slice(at, at + width)
            dst[0:3, lanes] = below[3:6]
            dst[3:9, lanes] = own[0:6]
            dst[9:12, lanes] = above[0:3]

    def split_rho(g):
        window = pl.ds(pl.multiple_of(g * 384, 384), 512)
        for src, base in ((xo, 0), (xz, 64)):
            block = src[:, window]
            for q in range(8):
                cbuf[g * 8 + q, :, base : base + BZ] = block[:, 112 + BZ * q : 112 + BZ * (q + 1)]

    loop(0, 4, split_rho, 4)
    source_row = iota((LANES, LANES), 0)
    fine_lane = iota((LANES, LANES), 1)
    fine_z = jnp.where(fine_lane >= LANES - M, fine_lane - LANES, fine_lane)
    coarse = jnp.where(source_row < 64, source_row, source_row - 64 + jnp.where(bk == 0, BZ, -BZ))
    real = (source_row < BZ) | ((source_row >= 64) & (source_row < 64 + BZ))
    odd = (fine_z + 128) % 2
    floor = (fine_z + 128) // 2 - 64
    wz = jnp.where(coarse == floor, 0.75 * math.pi, 0.0)
    wz = jnp.where(coarse == floor - 1 + 2 * odd, 0.25 * math.pi, wz)
    wz = jnp.where(real, wz, 0.0)
    fine = jnp.dot(
        cbuf[...].reshape(32 * 16, LANES), wz, precision=EXACT, preferred_element_type=F32
    ).reshape(32, 16, LANES)
    for y in range(30):
        f1[pl.ds(y + 5, 12, stride=40), :] = fine[y, 0:12]

    def refine_y(x):
        base = pl.multiple_of(x * 40, 8)
        block = f1[pl.ds(base, 40), :]
        mid = 0.75 * block[6:34]
        f2[x, pl.ds(4, 28, stride=2), :] = mid + 0.25 * block[5:33]
        f2[x, pl.ds(5, 28, stride=2), :] = mid + 0.25 * block[7:35]

    loop(0, 12, refine_y, 12)

    def refine_x(x):
        mid = 0.75 * f2[x]
        at = 2 * x - 1
        sa[at, span, :] = sa[at, span, :] + mid + 0.25 * f2[x - 1]
        sa[at + 1, span, :] = sa[at + 1, span, :] + mid + 0.25 * f2[x + 1]

    loop(1, 11, refine_x, 10)

    yrow = iota((SPAN, LANES), 0)
    y_ok = ((yrow >= 8) | has_ylo) & ((yrow < 8 + FY) | has_yhi)
    z_ok = (lane < FZ) | from_z
    sixth = jnp.where(y_ok & z_ok, 1.0 / 6.0, 0.0)
    x_low = jnp.where(has_xlo, 1.0, 0.0)
    x_high = jnp.where(has_xhi, 1.0, 0.0)

    for sweep in range(SWEEPS):
        old, new = (va, vb) if sweep % 2 == 0 else (vb, va)

        def update(x, old=old, new=new):
            mid = old[x, span, :]
            acc = old[x - 1, span, :] + old[x + 1, span, :] + sa[x, span, :]
            acc = acc + (old[x, Y0 - 9 : Y0 - 9 + SPAN, :] + old[x, Y0 - 7 : Y0 - 7 + SPAN, :])
            acc = acc + pltpu.roll(mid, 1, 1) + pltpu.roll(mid, LANES - 1, 1)
            factor = jnp.where(x < M, x_low, jnp.where(x >= M + FX, x_high, 1.0))
            new[x, span, :] = acc * (sixth * factor)

        loop(1 + sweep, NX - 1 - sweep, update, NX - 2 - 2 * sweep)

    for x in range(BX):
        at = 2 * x + M
        g3[x, 0:YROWS, :] = 0.125 * (va[at - 1] + va[at + 2]) + 0.375 * (va[at] + va[at + 1])
    for x in range(BX):
        c3[BY * x : BY * (x + 1), :] = 0.125 * (
            g3[x, pl.ds(Y0 - 1, BY, stride=2), :] + g3[x, pl.ds(Y0 + 2, BY, stride=2), :]
        ) + 0.375 * (g3[x, pl.ds(Y0, BY, stride=2), :] + g3[x, pl.ds(Y0 + 1, BY, stride=2), :])
    lane_in = iota((LANES, LANES), 0)
    cell = iota((LANES, LANES), 1)
    rel = jnp.where(lane_in == LANES - 1, -1, lane_in) - 2 * cell
    wr = jnp.where((rel == 0) | (rel == 1), 0.375, 0.0)
    wr = jnp.where((rel == -1) | (rel == 2), 0.125, wr)
    wr = jnp.where(cell < BZ, wr, 0.0)
    c3[...] = jnp.dot(c3[...], wr, precision=EXACT, preferred_element_type=F32)
    for y in range(BY):
        tmp_m[0:BX, y * BZ : (y + 1) * BZ] = c3[pl.ds(y, BX, stride=BY), :][:, 0:BZ]
    eff_out[...] = tmp_m[0:BX, :] + base[0:BX, :]

    def join(x):
        p0, p1, p2, p3 = (va[x + M, pl.ds(Y0 + q, 12, stride=4), :] for q in range(4))
        r0 = jnp.where(lane12 < 96, p0, pltpu.roll(p1, 96, 1))
        r1 = jnp.where(lane12 < 64, pltpu.roll(p1, 96, 1), pltpu.roll(p2, 64, 1))
        r2 = jnp.where(lane12 < 32, pltpu.roll(p2, 64, 1), pltpu.roll(p3, 32, 1))
        for r, val in enumerate((r0, r1, r2)):
            pot_out[pl.ds(36 * x + r, 12, stride=3), :] = val

    loop(0, FX, join, 6)

    finish()


def apply_kernel(stencil, effective, waves, potential, applied_out, potential_out, applied, sem):
    cp_pot = pltpu.make_async_copy(potential, potential_out, sem.at[BX])
    cp_pot.start()
    copies = []
    for x in range(BX):
        here = stencil[x] + effective[x : x + 1, :] * waves[x].astype(F32)
        applied[x] = here.astype(BF16)
        cp = pltpu.make_async_copy(applied.at[x], applied_out.at[x], sem.at[x])
        cp.start()
        copies.append(cp)
    for cp in copies:
        cp.wait()
    cp_pot.wait()


def solution(mesh):
    n_band = mesh.shape["band"]
    domains = mesh.shape["dom"]
    ny = min(4, domains // 4)
    nx = domains // (ny * 2)

    def local(orbitals, occupations, previous, compensation, local_potential):
        nb = orbitals.shape[0]
        hbm = pl.BlockSpec(memory_space=pltpu.HBM)
        vmem = pl.BlockSpec(memory_space=pltpu.VMEM)
        waves = orbitals[:, 0].transpose(1, 0, 2)
        stencil, effective, potential, held = pl.pallas_call(
            functools.partial(step_kernel, (nb, n_band, nx, ny)),
            out_shape=(
                jax.ShapeDtypeStruct((BX, nb, YZ), F32),
                jax.ShapeDtypeStruct((BX, YZ), F32),
                jax.ShapeDtypeStruct((OWN, LANES), F32),
                jax.ShapeDtypeStruct((BX, nb, YZ), BF16),
            ),
            in_specs=[hbm] * 5,
            out_specs=(vmem,) * 4,
            scratch_shapes=[
                pltpu.VMEM((nb, YZ), BF16),
                pltpu.VMEM((nb, YZ), BF16),
                pltpu.VMEM((BX, nb, YZ), BF16),
                pltpu.VMEM((BX, nb, LANES), BF16),
                pltpu.VMEM((BX, nb, LANES), BF16),
                pltpu.VMEM((1024, 384), BF16),
                pltpu.VMEM((1, nb), F32),
                pltpu.VMEM((nb, LANES), F32),
                pltpu.VMEM((2 * EDGE + OWN, LANES), F32),
                pltpu.VMEM((2 * EDGE + OWN, LANES), F32),
                pltpu.VMEM((OWN, LANES), BF16),
                pltpu.VMEM((OWN, LANES), BF16),
                pltpu.VMEM((2, EDGE, LANES), BF16),
                pltpu.VMEM((2, EDGE, LANES), BF16),
                pltpu.VMEM((BX, 1, YZ), F32),
            ]
            + [pltpu.VMEM((NX, YROWS, LANES), F32)] * 3
            + [
                pltpu.VMEM((2, 2, 48, LANES), F32),
                pltpu.VMEM((2, 2, 48, LANES), BF16),
                pltpu.VMEM((3, 2, 2, 48, LANES), BF16),
                pltpu.VMEM((2, 2, 88, LANES), F32),
                pltpu.VMEM((NX, SPAN, LANES), BF16),
                pltpu.VMEM((NX, SPAN, LANES), BF16),
                pltpu.VMEM((8, YZ), F32),
                pltpu.VMEM((n_band, 8, YZ), BF16),
                pltpu.VMEM((8, YZ), F32),
                pltpu.VMEM((8, YZ), BF16),
                pltpu.VMEM((18, 8, YZ), BF16),
                pltpu.VMEM((16, 512 + YZ), F32),
                pltpu.VMEM((16, 512 + YZ), F32),
                pltpu.VMEM((32, 16, LANES), F32),
                pltpu.VMEM((12 * 40, LANES), F32),
                pltpu.VMEM((12, SPAN, LANES), F32),
                pltpu.VMEM((BX, YROWS, LANES), F32),
                pltpu.VMEM((BX * BY, LANES), F32),
                pltpu.VMEM((8, YZ), F32),
                pltpu.VMEM((8, YZ), F32),
                pltpu.SemaphoreType.DMA((BX + 4,)),
                pltpu.SemaphoreType.DMA((N_SEM,)),
                pltpu.SemaphoreType.DMA((N_SEM,)),
            ],
            compiler_params=pltpu.CompilerParams(
                collective_id=0, has_side_effects=True, vmem_limit_bytes=48 * 1024 * 1024
            ),
        )(
            pltpu.with_memory_space_constraint(waves, pltpu.HBM),
            pltpu.with_memory_space_constraint(occupations.reshape(1, nb), pltpu.HBM),
            pltpu.with_memory_space_constraint(previous.reshape(OWN, LANES), pltpu.HBM),
            pltpu.with_memory_space_constraint(compensation.reshape(OWN, LANES), pltpu.HBM),
            pltpu.with_memory_space_constraint(local_potential.reshape(BX, 1, YZ), pltpu.HBM),
        )
        applied, potential = pl.pallas_call(
            apply_kernel,
            out_shape=(
                jax.ShapeDtypeStruct((BX, nb, YZ), BF16),
                jax.ShapeDtypeStruct((OWN, LANES), F32),
            ),
            in_specs=[vmem] * 4,
            out_specs=(hbm, hbm),
            scratch_shapes=[pltpu.VMEM((BX, nb, YZ), BF16), pltpu.SemaphoreType.DMA((BX + 1,))],
            compiler_params=pltpu.CompilerParams(vmem_limit_bytes=8 * 1024 * 1024),
        )(stencil, effective, held, potential)
        return applied.transpose(1, 0, 2)[:, None], potential.reshape(previous.shape)

    return jax.shard_map(
        local,
        mesh=mesh,
        in_specs=(
            P("band", "dom", None, None),
            P("band"),
            P("dom", None, None),
            P("dom", None, None),
            P("dom", None, None),
        ),
        out_specs=(P("band", "dom", None, None), P("dom", None, None)),
        check_vma=False,
    )
```

```python
import functools
import math

import jax
import jax.numpy as jnp
from jax import lax
from jax.experimental import pallas as pl
from jax.experimental.pallas import tpu as pltpu
from jax.sharding import PartitionSpec as P

BX, BY, BZ = 6, 24, 48
YZ = BY * BZ
FX, FY, FZ = 2 * BX, 2 * BY, 2 * BZ
FYZ = FY * FZ
BANDS = 768
SWEEPS = 4
M = 5
NX = FX + 2 * M
Y0 = 16
YROWS = FY + 2 * Y0
SPAN = FY + 16
EDGE = 192
OWN = FX * 36
LANES = 128
MESH = pl.DeviceIdType.MESH
F32, BF16 = jnp.float32, jnp.bfloat16
EXACT = lax.Precision.HIGHEST

OFFSETS = [
    (dx, dy, dz) for dx in (-1, 0, 1) for dy in (-1, 0, 1) for dz in (0, 1) if (dx, dy, dz) != (0, 0, 0)
]


def slot_of(dx, dy, dz):
    return ((dx + 1) * 3 + dy + 1) * 2 + dz


HALO = 0
BAND = 18
ORB_X, ORB_Y, ORB_Z = 26, 30, 32
POT_X, POT_Y, POT_Z = 33, 37, 43
N_SEM = 44


def loop(low, high, body, together):
    def some(step, carry):
        for u in range(together):
            body(low + step * together + u)
        return carry

    assert (high - low) % together == 0
    lax.fori_loop(0, (high - low) // together, some, 0)


def iota(shape, axis):
    return lax.broadcasted_iota(jnp.int32, shape, axis)


def step_kernel(
    sizes,
    orb, occ_in, prev_in, comp_in, loc_in,
    stencil, eff_out, pot_out, waves,
    xlo, xhi, zbuf, ylo, yhi, w_ref, occ, occ_col,
    pvx, cmx, send_v, send_c, edge_v, edge_c, loc,
    va, vb, sa, rim_tmp, rim_out, rim_in, rim_all, zsend, zrecv,
    part, gath, tot, totb, rh, xo, xz, cbuf, f1, f2, g3, c3, tmp_m, base,
    load_sem, send_sem, recv_sem,
):
    nb, n_band, nx, ny = sizes
    me = lax.axis_index("dom")
    band = lax.axis_index("band")
    bi = me // (ny * 2)
    bj = (me // 2) % ny
    bk = me % 2
    has_xlo, has_xhi = bi > 0, bi < nx - 1
    has_ylo, has_yhi = bj > 0, bj < ny - 1

    def exists(dx, dy):
        ok = None
        for flag in ([has_xlo] if dx < 0 else [has_xhi] if dx > 0 else []) + (
            [has_ylo] if dy < 0 else [has_yhi] if dy > 0 else []
        ):
            ok = flag if ok is None else jnp.logical_and(ok, flag)
        return ok

    def when(cond, fn):
        if cond is None:
            fn()
        else:
            pl.when(cond)(fn)

    def neighbour(dx, dy, dz):
        other = (1 - bk) if dz else bk
        return {"dom": ((bi + dx) * ny + bj + dy) * 2 + other, "band": band}

    def remote(src, dst, s_idx, r_idx, device):
        return pltpu.make_async_remote_copy(
            src_ref=src, dst_ref=dst, send_sem=send_sem.at[s_idx], recv_sem=recv_sem.at[r_idx],
            device_id=device, device_id_type=MESH,
        )

    leftovers = []

    def send(cp, where, arrival):
        when(where, cp.start)
        handle = [cp, arrival, False]
        leftovers.append((handle, where))
        return handle

    def arrive(*handles):
        for handle in handles:
            when(handle[1], handle[0].wait_recv)
            handle[2] = True

    def finish():
        for handle, where in leftovers:
            if not handle[2]:
                arrive(handle)
            when(where, handle[0].wait_send)

    cp_occ = pltpu.make_async_copy(occ_in, occ, load_sem.at[BX])
    cp_prev = pltpu.make_async_copy(prev_in, pvx.at[pl.ds(EDGE, OWN)], load_sem.at[BX + 1])
    cp_comp = pltpu.make_async_copy(comp_in, cmx.at[pl.ds(EDGE, OWN)], load_sem.at[BX + 2])
    cp_loc = pltpu.make_async_copy(loc_in, loc, load_sem.at[BX + 3])
    loads = [pltpu.make_async_copy(orb.at[x], waves.at[x], load_sem.at[x]) for x in range(BX)]
    cp_occ.start()
    for cp in loads:
        cp.start()
    cp_prev.start()
    cp_comp.start()
    cp_loc.start()

    barrier = pltpu.get_barrier_semaphore()
    for d in range(1, n_band):
        pl.semaphore_signal(
            barrier, inc=1, device_id={"dom": me, "band": (band + d) % n_band}, device_id_type=MESH
        )
    for dx, dy, dz in OFFSETS:
        def greet(dx=dx, dy=dy, dz=dz):
            pl.semaphore_signal(barrier, inc=1, device_id=neighbour(dx, dy, dz), device_id_type=MESH)
        when(exists(dx, dy), greet)

    cp_occ.wait()
    diagonal = jnp.where(iota((nb, nb), 0) == iota((nb, nb), 1), occ[...] * (1.0 / BANDS), 0.0)
    occ_col[...] = jnp.broadcast_to(jnp.sum(diagonal, 1, keepdims=True), (nb, LANES))

    part[...] = jnp.zeros((8, YZ), F32)
    base[...] = jnp.zeros((8, YZ), F32)
    for x in range(BX):
        loads[x].wait()

        for blk in range(YZ // LANES):
            cols = slice(LANES * blk, LANES * (blk + 1))
            wave = waves[x, :, cols].astype(F32)
            part[x : x + 1, cols] = jnp.sum((wave * occ_col[...]) * wave, 0, keepdims=True)

    def packed(field):
        mean = (jnp.sum(field, 0, keepdims=True) * (1.0 / BX)).astype(BF16).astype(F32)
        row = iota(field.shape, 0)
        return jnp.where(row < BX, field - mean, jnp.where(row == BX, mean, 0.0)).astype(BF16)

    def unpacked(block):
        return block + block[BX : BX + 1]

    gath[band] = packed(part[...])

    one = lambda flag: jnp.where(flag, 1, 0)
    n_dom = (1 + one(has_xlo) + one(has_xhi)) * (1 + one(has_ylo) + one(has_yhi)) * 2 - 1
    pl.semaphore_wait(barrier, n_dom + n_band - 1)
    band_in = [
        send(
            remote(gath.at[band], gath.at[band], BAND + d, BAND + d, {"dom": me, "band": (band + d) % n_band}),
            None, None,
        )
        for d in sorted(range(1, n_band), key=lambda d: -min(d, n_band - d))
    ]

    cp_prev.wait()
    cp_comp.wait()
    cp_loc.wait()
    send_v[...] = pvx[EDGE : EDGE + OWN, :].astype(BF16)
    send_c[...] = cmx[EDGE : EDGE + OWN, :].astype(BF16)
    px_in = []
    for n, (src, dst) in enumerate(((send_v, edge_v), (send_c, edge_c))):
        px_in.append(send(
            remote(src.at[pl.ds(0, EDGE)], dst.at[0], POT_X + 2 * n, POT_X + 2 * n, neighbour(-1, 0, 0)),
            has_xlo, has_xhi,
        ))
        px_in.append(send(
            remote(
                src.at[pl.ds(OWN - EDGE, EDGE)], dst.at[1], POT_X + 2 * n + 1, POT_X + 2 * n + 1, neighbour(1, 0, 0)
            ),
            has_xhi, has_xlo,
        ))

    for x in range(FX):
        for n, src in enumerate((pvx, cmx)):
            at = EDGE + 36 * x
            rim_tmp[0, n, 4 * x : 4 * x + 4, :] = src[at : at + 4, :]
            rim_tmp[1, n, 4 * x : 4 * x + 4, :] = src[at + 32 : at + 36, :]
    rim_out[...] = rim_tmp[:, :, 0:48, :].astype(BF16)
    rim_copies = []
    for side, dy in ((0, -1), (1, 1)):
        for dx in (0, -1, 1):
            rows = {0: pl.ds(0, 48), -1: pl.ds(0, 32), 1: pl.ds(16, 32)}[dx]
            cp = remote(
                rim_out.at[side, :, rows], rim_in.at[1 - dx, side, :, rows],
                POT_Y + 3 * side + dx + 1, POT_Y + 3 * side + dx + 1, neighbour(dx, dy, 0),
            )
            rim_copies.append(send(cp, exists(dx, dy), exists(-dx, -dy)))

    half = pl.ds(0, nb // 2), pl.ds(nb // 2, nb // 2)

    def orbitals_along_x(n):
        return [
            send(
                remote(orb.at[0, half[n]], xhi.at[half[n]], ORB_X + 2 * n, ORB_X + 2 * n, neighbour(-1, 0, 0)),
                has_xlo, has_xhi,
            ),
            send(
                remote(
                    orb.at[BX - 1, half[n]], xlo.at[half[n]], ORB_X + 2 * n + 1, ORB_X + 2 * n + 1, neighbour(1, 0, 0)
                ),
                has_xhi, has_xlo,
            ),
        ]

    orb_in = [
        send(
            remote(orb.at[:, :, pl.ds(0, LANES)], yhi, ORB_Y, ORB_Y, neighbour(0, -1, 0)), has_ylo, has_yhi
        ),
        send(
            remote(orb.at[:, :, pl.ds(YZ - LANES, LANES)], ylo, ORB_Y + 1, ORB_Y + 1, neighbour(0, 1, 0)),
            has_yhi, has_ylo,
        ),
        send(remote(orb, zbuf, ORB_Z, ORB_Z, neighbour(0, 0, 1)), None, None),
    ]
    orb_x_in = orbitals_along_x(0)

    def zero(ref, *index):
        def run():
            view = ref.at[index] if index else ref
            view[...] = jnp.zeros(view.shape, view.dtype)
        return run

    when(jnp.logical_not(has_xhi), zero(xhi))
    when(jnp.logical_not(has_xlo), zero(xlo))
    for ref in (edge_v, edge_c):
        when(jnp.logical_not(has_xhi), zero(ref, 0))
        when(jnp.logical_not(has_xlo), zero(ref, 1))
    when(jnp.logical_not(has_ylo), zero(ylo))
    when(jnp.logical_not(has_yhi), zero(yhi))
    for dx, dy, dz in OFFSETS:
        cond = exists(dx, dy)
        if cond is not None:
            when(jnp.logical_not(cond), zero(rh, slot_of(dx, dy, dz)))
    for side, dy in ((0, -1), (1, 1)):
        for dx in (-1, 0, 1):
            when(jnp.logical_not(exists(-dx, -dy)), zero(rim_in, 1 - dx, side))
    for x in range(NX):
        for ref in (va, vb, sa):
            ref[x, 0:Y0, :] = jnp.zeros((Y0, LANES), F32)
            ref[x, Y0 + FY :, :] = jnp.zeros((Y0, LANES), F32)
    cbuf[...] = jnp.zeros(cbuf.shape, F32)
    xo[...] = jnp.zeros(xo.shape, F32)
    xz[...] = jnp.zeros(xz.shape, F32)

    def fill_w(r, carry):
        row = iota((LANES, 384), 0) + r * LANES
        col = iota((LANES, 384), 1)
        place = iota((1, 384), 1) % BZ
        diff = row - LANES - col
        main = jnp.where(diff == 0, 3.0, 0.0)
        side = (
            (diff == BZ) | (diff == -BZ)
            | ((diff == 1) & (place != BZ - 1)) | ((diff == -1) & (place != 0))
        )
        main = jnp.where(side, -0.5, main)
        far = row - 640 - col
        over = jnp.where(
            bk == 0,
            jnp.where((far == 1 - BZ) & (place == BZ - 1), -0.5, 0.0),
            jnp.where((far == BZ - 1) & (place == 0), -0.5, 0.0),
        )
        w_ref[pl.ds(pl.multiple_of(r * LANES, LANES), LANES), :] = jnp.where(row < 640, main, over).astype(BF16)
        return carry

    lax.fori_loop(0, 8, fill_w, 0)

    lane12 = iota((12, LANES), 1)

    def thread(a0, a1, a2, lanes):
        y0 = a0
        y1 = jnp.where(lanes < 32, pltpu.roll(a0, 32, 1), pltpu.roll(a1, 32, 1))
        y2 = jnp.where(lanes < 64, pltpu.roll(a1, 64, 1), pltpu.roll(a2, 64, 1))
        y3 = pltpu.roll(a2, 96, 1)
        return [jnp.where(lanes < FZ, val, 0.0) for val in (y0, y1, y2, y3)]

    fields = ((pvx, va, 1.0), (cmx, sa, -math.pi))

    def split(x):
        base = EDGE - 36 * M + 36 * x
        for src, dst, scale in fields:
            rows = [scale * src[pl.ds(base + r, 12, stride=3), :] for r in range(3)]
            for q, val in enumerate(thread(*rows, lane12)):
                dst[x, pl.ds(Y0 + q, 12, stride=4), :] = val

    loop(M, M + FX, split, 6)

    arrive(*band_in)
    rho = gath[0].astype(F32)
    for d in range(1, n_band):
        rho = rho + gath[d].astype(F32)
    rho = jnp.where(iota((8, YZ), 0) < BX, unpacked(rho), 0.0)
    tot[...] = rho
    totb[...] = packed(rho)
    halo_in = []
    for dx, dy, dz in sorted(OFFSETS, key=lambda o: (-abs(o[0]) - abs(o[1]), -abs(o[0]), -o[2])):
        there = slot_of(-dx, -dy, dz)
        cols = {0: pl.ds(0, YZ), -1: pl.ds(0, 256), 1: pl.ds(YZ - 256, 256)}[dy]
        cp = remote(
            totb.at[:, cols], rh.at[there, :, cols], HALO + slot_of(dx, dy, dz), HALO + there,
            neighbour(dx, dy, dz),
        )
        halo_in.append(send(cp, exists(dx, dy), exists(-dx, -dy)))

    orb_x_in = orb_x_in + orbitals_along_x(1)

    arrive(*px_in)
    for full, edge in ((pvx, edge_v), (cmx, edge_c)):
        full[EDGE + OWN : 2 * EDGE + OWN, :] = edge[0].astype(F32)
        full[0:EDGE, :] = edge[1].astype(F32)
    loop(0, M, split, 5)
    loop(M + FX, NX, split, 5)
    arrive(*rim_copies)
    lane22 = iota((NX, LANES), 1)
    for n, (_, dst, scale) in enumerate(fields):
        flat = dst.reshape((NX + 2) * YROWS, LANES)
        for side in range(2):
            rim_tmp[0, 0, 0:20, :] = rim_in[0, side, n].astype(F32)[28:48]
            rim_tmp[0, 0, 20:48, :] = rim_in[1, side, n].astype(F32)[0:28]
            rim_tmp[0, 1, 0:20, :] = rim_in[1, side, n].astype(F32)[28:48]
            rim_tmp[0, 1, 20:40, :] = rim_in[2, side, n].astype(F32)[0:20]
            rim_all[side, n, 0:48, :] = rim_tmp[0, 0, 0:48, :]
            rim_all[side, n, 48:88, :] = rim_tmp[0, 1, 0:40, :]
            a = [scale * rim_all[side, n, pl.ds(r, NX, stride=4), :] for r in range(4)]
            if side == 0:
                cells = [*thread(a[0], a[1], a[2], lane22), jnp.where(lane22 < FZ, a[3], 0.0)]
                first = Y0 + FY
            else:
                cells = [jnp.where(lane22 < FZ, pltpu.roll(a[0], 96, 1), 0.0), *thread(a[1], a[2], a[3], lane22)]
                first = Y0 - M
            for q, val in enumerate(cells):
                flat[pl.ds(first + q, NX, stride=YROWS), :] = val

    lane = iota((SPAN, LANES), 1)
    span = slice(Y0 - 8, Y0 - 8 + SPAN)
    inner = (lane < M) | ((lane >= 64) & (lane < 64 + M))

    def pack_z(x):
        v, s = va[x, span, :], sa[x, span, :]
        first = jnp.where(lane < 64, v, pltpu.roll(s, 64, 1))
        last = jnp.where(lane < 64, pltpu.roll(v, 16 + M - FZ + LANES, 1), pltpu.roll(s, 80 + M - FZ + LANES, 1))
        zsend[x] = jnp.where(inner, first, last).astype(BF16)

    loop(0, NX, pack_z, 11)
    z_in = send(remote(zsend, zrecv, POT_Z, POT_Z, neighbour(0, 0, 1)), None, None)

    for x in range(BX):
        base[x : x + 1, :] = loc[x]
    base[...] = base[...] - jnp.exp(jnp.log((3.0 / math.pi) * tot[...]) * (1.0 / 3.0))

    arrive(*orb_in)
    for first in (0, 3):
        group = slice(first, first + 3)
        for t in range(3):
            if t == 0:
                here = [ylo[group], waves[group, :, 0:512]]
            elif t == 1:
                here = [waves[group, :, 256:896]]
            else:
                here = [waves[group, :, 640:1152], yhi[group]]
            cols = slice(384 * t, 384 * (t + 1))
            lhs = jnp.concatenate([*here, zbuf[group, :, cols]], 2).reshape(3 * nb, 1024)
            out = jnp.dot(lhs, w_ref[...], preferred_element_type=F32).reshape(3, nb, 384)
            for u in range(3):
                x = first + u
                sides = [waves[other, :, cols].astype(F32) for other in (x - 1, x + 1) if 0 <= other < BX]
                stencil[x, :, cols] = out[u] - 0.5 * sum(sides[1:], sides[0])

    arrive(z_in)
    from_z = jnp.where(bk == 0, jnp.where((lane >= FZ) & (lane < FZ + M), 1, 0), jnp.where(lane >= LANES - M, 1, 0)) == 1
    shift_v = jnp.where(bk == 0, FZ, LANES - M - 16)
    shift_s = jnp.where(bk == 0, FZ - 64, 64 - M - 16)

    def merge(x):
        rim = zrecv[x].astype(F32)
        va[x, span, :] = jnp.where(from_z, pltpu.roll(rim, shift_v, 1), va[x, span, :])
        sa[x, span, :] = jnp.where(from_z, pltpu.roll(rim, shift_s, 1), sa[x, span, :])

    loop(0, NX, merge, 11)


    arrive(*halo_in)
    for dst, dz in ((xo, 0), (xz, 1)):
        for dy, start, width, at in ((0, 0, YZ, 256), (-1, YZ - 256, 256, 0), (1, 0, 256, 256 + YZ)):
            cols = slice(start, start + width)
            own = tot[...] if dz == 0 and dy == 0 else unpacked(rh[slot_of(0, dy, dz), :, cols].astype(F32))
            above = unpacked(rh[slot_of(1, dy, dz), :, cols].astype(F32))
            below = unpacked(rh[slot_of(-1, dy, dz), :, cols].astype(F32))
            lanes = slice(at, at + width)
            dst[0:3, lanes] = below[3:6]
            dst[3:9, lanes] = own[0:6]
            dst[9:12, lanes] = above[0:3]

    def split_rho(g):
        window = pl.ds(pl.multiple_of(g * 384, 384), 512)
        for src, base in ((xo, 0), (xz, 64)):
            block = src[:, window]
            for q in range(8):
                cbuf[g * 8 + q, :, base : base + BZ] = block[:, 112 + BZ * q : 112 + BZ * (q + 1)]

    loop(0, 4, split_rho, 4)
    source_row = iota((LANES, LANES), 0)
    fine_lane = iota((LANES, LANES), 1)
    fine_z = jnp.where(fine_lane >= LANES - M, fine_lane - LANES, fine_lane)
    coarse = jnp.where(source_row < 64, source_row, source_row - 64 + jnp.where(bk == 0, BZ, -BZ))
    real = (source_row < BZ) | ((source_row >= 64) & (source_row < 64 + BZ))
    odd = (fine_z + 128) % 2
    floor = (fine_z + 128) // 2 - 64
    wz = jnp.where(coarse == floor, 0.75 * math.pi, 0.0)
    wz = jnp.where(coarse == floor - 1 + 2 * odd, 0.25 * math.pi, wz)
    wz = jnp.where(real, wz, 0.0)
    fine = jnp.dot(
        cbuf[...].reshape(32 * 16, LANES), wz, precision=EXACT, preferred_element_type=F32
    ).reshape(32, 16, LANES)
    for y in range(30):
        f1[pl.ds(y + 5, 12, stride=40), :] = fine[y, 0:12]

    def refine_y(x):
        base = pl.multiple_of(x * 40, 8)
        block = f1[pl.ds(base, 40), :]
        mid = 0.75 * block[6:34]
        f2[x, pl.ds(4, 28, stride=2), :] = mid + 0.25 * block[5:33]
        f2[x, pl.ds(5, 28, stride=2), :] = mid + 0.25 * block[7:35]

    loop(0, 12, refine_y, 12)

    def refine_x(x):
        mid = 0.75 * f2[x, 0:SPAN, :]
        at = 2 * x - 1
        sa[at, span, :] = sa[at, span, :] + mid + 0.25 * f2[x - 1, 0:SPAN, :]
        sa[at + 1, span, :] = sa[at + 1, span, :] + mid + 0.25 * f2[x + 1, 0:SPAN, :]

    loop(1, 11, refine_x, 10)

    yrow = iota((SPAN, LANES), 0)
    y_ok = ((yrow >= 8) | has_ylo) & ((yrow < 8 + FY) | has_yhi)
    z_ok = (lane < FZ) | from_z
    sixth = jnp.where(y_ok & z_ok, 1.0 / 6.0, 0.0)
    x_low = jnp.where(has_xlo, 1.0, 0.0)
    x_high = jnp.where(has_xhi, 1.0, 0.0)

    for sweep in range(SWEEPS):
        old, new = (va, vb) if sweep % 2 == 0 else (vb, va)

        def update(x, old=old, new=new):
            mid = old[x, span, :]
            acc = old[x - 1, span, :] + old[x + 1, span, :] + sa[x, span, :]
            acc = acc + (old[x, Y0 - 9 : Y0 - 9 + SPAN, :] + old[x, Y0 - 7 : Y0 - 7 + SPAN, :])
            acc = acc + pltpu.roll(mid, 1, 1) + pltpu.roll(mid, LANES - 1, 1)
            factor = jnp.where(x < M, x_low, jnp.where(x >= M + FX, x_high, 1.0))
            new[x, span, :] = acc * (sixth * factor)

        loop(1 + sweep, NX - 1 - sweep, update, NX - 2 - 2 * sweep)

    arrive(*orb_x_in)
    stencil[0] = stencil[0] - 0.5 * xlo[...].astype(F32)
    stencil[BX - 1] = stencil[BX - 1] - 0.5 * xhi[...].astype(F32)

    for x in range(BX):
        at = 2 * x + M
        g3[x, 0:YROWS, :] = 0.125 * (va[at - 1] + va[at + 2]) + 0.375 * (va[at] + va[at + 1])
    for x in range(BX):
        c3[BY * x : BY * (x + 1), :] = 0.125 * (
            g3[x, pl.ds(Y0 - 1, BY, stride=2), :] + g3[x, pl.ds(Y0 + 2, BY, stride=2), :]
        ) + 0.375 * (g3[x, pl.ds(Y0, BY, stride=2), :] + g3[x, pl.ds(Y0 + 1, BY, stride=2), :])
    lane_in = iota((LANES, LANES), 0)
    cell = iota((LANES, LANES), 1)
    rel = jnp.where(lane_in == LANES - 1, -1, lane_in) - 2 * cell
    wr = jnp.where((rel == 0) | (rel == 1), 0.375, 0.0)
    wr = jnp.where((rel == -1) | (rel == 2), 0.125, wr)
    wr = jnp.where(cell < BZ, wr, 0.0)
    c3[0 : BX * BY, :] = jnp.dot(c3[0 : BX * BY, :], wr, precision=EXACT, preferred_element_type=F32)
    for y in range(BY):
        tmp_m[0:BX, y * BZ : (y + 1) * BZ] = c3[pl.ds(y, BX, stride=BY), :][:, 0:BZ]
    eff_out[...] = tmp_m[0:BX, :] + base[0:BX, :]

    def join(x):
        p0, p1, p2, p3 = (va[x + M, pl.ds(Y0 + q, 12, stride=4), :] for q in range(4))
        r0 = jnp.where(lane12 < 96, p0, pltpu.roll(p1, 96, 1))
        r1 = jnp.where(lane12 < 64, pltpu.roll(p1, 96, 1), pltpu.roll(p2, 64, 1))
        r2 = jnp.where(lane12 < 32, pltpu.roll(p2, 64, 1), pltpu.roll(p3, 32, 1))
        for r, val in enumerate((r0, r1, r2)):
            pot_out[pl.ds(36 * x + r, 12, stride=3), :] = val

    loop(0, FX, join, 6)

    finish()


def apply_kernel(stencil, effective, waves, potential, applied_out, potential_out, applied, sem):
    cp_pot = pltpu.make_async_copy(potential.at[pl.ds(0, OWN)], potential_out, sem.at[BX])
    cp_pot.start()
    copies = []
    for x in range(BX):
        here = stencil[x] + effective[x : x + 1, :] * waves[x].astype(F32)
        applied[x] = here.astype(BF16)
        cp = pltpu.make_async_copy(applied.at[x], applied_out.at[x], sem.at[x])
        cp.start()
        copies.append(cp)
    for cp in copies:
        cp.wait()
    cp_pot.wait()


def solution(mesh):
    n_band = mesh.shape["band"]
    domains = mesh.shape["dom"]
    ny = min(4, domains // 4)
    nx = domains // (ny * 2)

    def local(orbitals, occupations, previous, compensation, local_potential):
        nb = orbitals.shape[0]
        hbm = pl.BlockSpec(memory_space=pltpu.HBM)
        vmem = pl.BlockSpec(memory_space=pltpu.VMEM)
        waves = orbitals[:, 0].transpose(1, 0, 2)
        stencil, effective, potential, held = pl.pallas_call(
            functools.partial(step_kernel, (nb, n_band, nx, ny)),
            out_shape=(
                jax.ShapeDtypeStruct((BX, nb, YZ), F32),
                jax.ShapeDtypeStruct((BX, YZ), F32),
                jax.ShapeDtypeStruct((OWN + 16, LANES), F32),
                jax.ShapeDtypeStruct((BX, nb, YZ), BF16),
            ),
            in_specs=[hbm] * 5,
            out_specs=(vmem,) * 4,
            scratch_shapes=[
                pltpu.VMEM((nb, YZ), BF16),
                pltpu.VMEM((nb, YZ), BF16),
                pltpu.VMEM((BX, nb, YZ), BF16),
                pltpu.VMEM((BX, nb, LANES), BF16),
                pltpu.VMEM((BX, nb, LANES), BF16),
                pltpu.VMEM((1024, 384), BF16),
                pltpu.VMEM((1, nb), F32),
                pltpu.VMEM((nb, LANES), F32),
                pltpu.VMEM((2 * EDGE + OWN, LANES), F32),
                pltpu.VMEM((2 * EDGE + OWN, LANES), F32),
                pltpu.VMEM((OWN, LANES), BF16),
                pltpu.VMEM((OWN, LANES), BF16),
                pltpu.VMEM((2, EDGE, LANES), BF16),
                pltpu.VMEM((2, EDGE, LANES), BF16),
                pltpu.VMEM((BX, 1, YZ), F32),
            ]
            + [pltpu.VMEM((NX + 2, YROWS, LANES), F32)] * 3
            + [
                pltpu.VMEM((2, 2, 56, LANES), F32),
                pltpu.VMEM((2, 2, 48, LANES), BF16),
                pltpu.VMEM((3, 2, 2, 48, LANES), BF16),
                pltpu.VMEM((2, 2, 96, LANES), F32),
                pltpu.VMEM((NX, SPAN, LANES), BF16),
                pltpu.VMEM((NX, SPAN, LANES), BF16),
                pltpu.VMEM((8, YZ), F32),
                pltpu.VMEM((n_band, 8, YZ), BF16),
                pltpu.VMEM((8, YZ), F32),
                pltpu.VMEM((8, YZ), BF16),
                pltpu.VMEM((18, 8, YZ), BF16),
                pltpu.VMEM((16, 512 + YZ), F32),
                pltpu.VMEM((16, 512 + YZ), F32),
                pltpu.VMEM((32, 16, LANES), F32),
                pltpu.VMEM((16 * 40, LANES), F32),
                pltpu.VMEM((12, SPAN + 8, LANES), F32),
                pltpu.VMEM((BX, YROWS, LANES), F32),
                pltpu.VMEM((8 * BY, LANES), F32),
                pltpu.VMEM((8, YZ), F32),
                pltpu.VMEM((8, YZ), F32),
                pltpu.SemaphoreType.DMA((BX + 4,)),
                pltpu.SemaphoreType.DMA((N_SEM,)),
                pltpu.SemaphoreType.DMA((N_SEM,)),
            ],
            compiler_params=pltpu.CompilerParams(
                collective_id=0, has_side_effects=True, vmem_limit_bytes=48 * 1024 * 1024
            ),
        )(
            pltpu.with_memory_space_constraint(waves, pltpu.HBM),
            pltpu.with_memory_space_constraint(occupations.reshape(1, nb), pltpu.HBM),
            pltpu.with_memory_space_constraint(previous.reshape(OWN, LANES), pltpu.HBM),
            pltpu.with_memory_space_constraint(compensation.reshape(OWN, LANES), pltpu.HBM),
            pltpu.with_memory_space_constraint(local_potential.reshape(BX, 1, YZ), pltpu.HBM),
        )
        applied, potential = pl.pallas_call(
            apply_kernel,
            out_shape=(
                jax.ShapeDtypeStruct((BX, nb, YZ), BF16),
                jax.ShapeDtypeStruct((OWN, LANES), F32),
            ),
            in_specs=[vmem] * 4,
            out_specs=(hbm, hbm),
            scratch_shapes=[pltpu.VMEM((BX, nb, YZ), BF16), pltpu.SemaphoreType.DMA((BX + 1,))],
            compiler_params=pltpu.CompilerParams(vmem_limit_bytes=8 * 1024 * 1024),
        )(stencil, effective, held, potential)
        return applied.transpose(1, 0, 2)[:, None], potential.reshape(previous.shape)

    return jax.shard_map(
        local,
        mesh=mesh,
        in_specs=(
            P("band", "dom", None, None),
            P("band"),
            P("dom", None, None),
            P("dom", None, None),
            P("dom", None, None),
        ),
        out_specs=(P("band", "dom", None, None), P("dom", None, None)),
        check_vma=False,
    )
```

```python
import functools
import math

import jax
import jax.numpy as jnp
from jax import lax
from jax.experimental import pallas as pl
from jax.experimental.pallas import tpu as pltpu
from jax.sharding import PartitionSpec as P

BX, BY, BZ = 6, 24, 48
YZ = BY * BZ
FX, FY, FZ = 2 * BX, 2 * BY, 2 * BZ
FYZ = FY * FZ
BANDS = 768
SWEEPS = 4
M = 5
NX = FX + 2 * M
Y0 = 16
YROWS = FY + 2 * Y0
SPAN = FY + 16
EDGE = 192
OWN = FX * 36
LANES = 128
MESH = pl.DeviceIdType.MESH
F32, BF16 = jnp.float32, jnp.bfloat16
EXACT = lax.Precision.HIGHEST

OFFSETS = [
    (dx, dy, dz) for dx in (-1, 0, 1) for dy in (-1, 0, 1) for dz in (0, 1) if (dx, dy, dz) != (0, 0, 0)
]


def slot_of(dx, dy, dz):
    return ((dx + 1) * 3 + dy + 1) * 2 + dz


HALO = 0
BAND = 18
ORB_X, ORB_Y, ORB_Z = 26, 30, 32
POT_X, POT_Y, POT_Z = 33, 37, 43
N_SEM = 44


def loop(low, high, body, together):
    def some(step, carry):
        for u in range(together):
            body(low + step * together + u)
        return carry

    assert (high - low) % together == 0
    if together == high - low:
        for i in range(low, high):
            body(i)
        return
    lax.fori_loop(0, (high - low) // together, some, 0)


def iota(shape, axis):
    return lax.broadcasted_iota(jnp.int32, shape, axis)


def step_kernel(
    sizes,
    orb, occ_in, prev_in, comp_in, loc_in,
    stencil, eff_out, pot_out, waves,
    xlo, xhi, zbuf, ylo, yhi, w_ref, occ, occ_col,
    pvx, cmx, send_v, send_c, edge_v, edge_c, loc,
    va, vb, sa, rim_tmp, rim_out, rim_in, rim_all, zsend, zrecv,
    part, gath, tot, totb, rh, xo, xz, cbuf, f1, f2, g3, c3, tmp_m, base,
    load_sem, send_sem, recv_sem,
):
    nb, n_band, nx, ny = sizes
    me = lax.axis_index("dom")
    band = lax.axis_index("band")
    bi = me // (ny * 2)
    bj = (me // 2) % ny
    bk = me % 2
    has_xlo, has_xhi = bi > 0, bi < nx - 1
    has_ylo, has_yhi = bj > 0, bj < ny - 1

    def exists(dx, dy):
        ok = None
        for flag in ([has_xlo] if dx < 0 else [has_xhi] if dx > 0 else []) + (
            [has_ylo] if dy < 0 else [has_yhi] if dy > 0 else []
        ):
            ok = flag if ok is None else jnp.logical_and(ok, flag)
        return ok

    def when(cond, fn):
        if cond is None:
            fn()
        else:
            pl.when(cond)(fn)

    def neighbour(dx, dy, dz):
        other = (1 - bk) if dz else bk
        return {"dom": ((bi + dx) * ny + bj + dy) * 2 + other, "band": band}

    def remote(src, dst, s_idx, r_idx, device):
        return pltpu.make_async_remote_copy(
            src_ref=src, dst_ref=dst, send_sem=send_sem.at[s_idx], recv_sem=recv_sem.at[r_idx],
            device_id=device, device_id_type=MESH,
        )

    leftovers = []

    def send(cp, where, arrival):
        when(where, cp.start)
        handle = [cp, arrival, False]
        leftovers.append((handle, where))
        return handle

    def arrive(*handles):
        for handle in handles:
            when(handle[1], handle[0].wait_recv)
            handle[2] = True

    def finish():
        for handle, where in leftovers:
            if not handle[2]:
                arrive(handle)
            when(where, handle[0].wait_send)

    cp_occ = pltpu.make_async_copy(occ_in, occ, load_sem.at[BX])
    cp_prev = pltpu.make_async_copy(prev_in, pvx.at[pl.ds(EDGE, OWN)], load_sem.at[BX + 1])
    cp_comp = pltpu.make_async_copy(comp_in, cmx.at[pl.ds(EDGE, OWN)], load_sem.at[BX + 2])
    cp_loc = pltpu.make_async_copy(loc_in, loc, load_sem.at[BX + 3])
    loads = [pltpu.make_async_copy(orb.at[x], waves.at[x], load_sem.at[x]) for x in range(BX)]
    cp_occ.start()
    for cp in loads:
        cp.start()
    cp_prev.start()
    cp_comp.start()
    cp_loc.start()

    barrier = pltpu.get_barrier_semaphore()
    for d in range(1, n_band):
        pl.semaphore_signal(
            barrier, inc=1, device_id={"dom": me, "band": (band + d) % n_band}, device_id_type=MESH
        )
    for dx, dy, dz in OFFSETS:
        def greet(dx=dx, dy=dy, dz=dz):
            pl.semaphore_signal(barrier, inc=1, device_id=neighbour(dx, dy, dz), device_id_type=MESH)
        when(exists(dx, dy), greet)

    cp_occ.wait()
    diagonal = jnp.where(iota((nb, nb), 0) == iota((nb, nb), 1), occ[...] * (1.0 / BANDS), 0.0)
    occ_col[...] = jnp.broadcast_to(jnp.sum(diagonal, 1, keepdims=True), (nb, LANES))

    part[...] = jnp.zeros((8, YZ), F32)
    base[...] = jnp.zeros((8, YZ), F32)
    for x in range(BX):
        loads[x].wait()

        for blk in range(YZ // LANES):
            cols = slice(LANES * blk, LANES * (blk + 1))
            wave = waves[x, :, cols].astype(F32)
            part[x : x + 1, cols] = jnp.sum((wave * occ_col[...]) * wave, 0, keepdims=True)

    def packed(field):
        mean = (jnp.sum(field, 0, keepdims=True) * (1.0 / BX)).astype(BF16).astype(F32)
        row = iota(field.shape, 0)
        return jnp.where(row < BX, field - mean, jnp.where(row == BX, mean, 0.0)).astype(BF16)

    def unpacked(block):
        return block + block[BX : BX + 1]

    gath[band] = packed(part[...])

    one = lambda flag: jnp.where(flag, 1, 0)
    n_dom = (1 + one(has_xlo) + one(has_xhi)) * (1 + one(has_ylo) + one(has_yhi)) * 2 - 1
    pl.semaphore_wait(barrier, n_dom + n_band - 1)
    band_in = [
        send(
            remote(gath.at[band], gath.at[band], BAND + d, BAND + d, {"dom": me, "band": (band + d) % n_band}),
            None, None,
        )
        for d in sorted(range(1, n_band), key=lambda d: -min(d, n_band - d))
    ]

    cp_prev.wait()
    cp_comp.wait()
    cp_loc.wait()
    send_v[...] = pvx[EDGE : EDGE + OWN, :].astype(BF16)
    send_c[...] = cmx[EDGE : EDGE + OWN, :].astype(BF16)
    px_in = []
    for n, (src, dst) in enumerate(((send_v, edge_v), (send_c, edge_c))):
        px_in.append(send(
            remote(src.at[pl.ds(0, EDGE)], dst.at[0], POT_X + 2 * n, POT_X + 2 * n, neighbour(-1, 0, 0)),
            has_xlo, has_xhi,
        ))
        px_in.append(send(
            remote(
                src.at[pl.ds(OWN - EDGE, EDGE)], dst.at[1], POT_X + 2 * n + 1, POT_X + 2 * n + 1, neighbour(1, 0, 0)
            ),
            has_xhi, has_xlo,
        ))

    for x in range(FX):
        for n, src in enumerate((pvx, cmx)):
            at = EDGE + 36 * x
            rim_tmp[0, n, 4 * x : 4 * x + 4, :] = src[at : at + 4, :]
            rim_tmp[1, n, 4 * x : 4 * x + 4, :] = src[at + 32 : at + 36, :]
    rim_out[...] = rim_tmp[:, :, 0:48, :].astype(BF16)
    rim_copies = []
    for side, dy in ((0, -1), (1, 1)):
        for dx in (0, -1, 1):
            rows = {0: pl.ds(0, 48), -1: pl.ds(0, 32), 1: pl.ds(16, 32)}[dx]
            cp = remote(
                rim_out.at[side, :, rows], rim_in.at[1 - dx, side, :, rows],
                POT_Y + 3 * side + dx + 1, POT_Y + 3 * side + dx + 1, neighbour(dx, dy, 0),
            )
            rim_copies.append(send(cp, exists(dx, dy), exists(-dx, -dy)))

    half = pl.ds(0, nb // 2), pl.ds(nb // 2, nb // 2)

    def orbitals_along_x(n):
        return [
            send(
                remote(orb.at[0, half[n]], xhi.at[half[n]], ORB_X + 2 * n, ORB_X + 2 * n, neighbour(-1, 0, 0)),
                has_xlo, has_xhi,
            ),
            send(
                remote(
                    orb.at[BX - 1, half[n]], xlo.at[half[n]], ORB_X + 2 * n + 1, ORB_X + 2 * n + 1, neighbour(1, 0, 0)
                ),
                has_xhi, has_xlo,
            ),
        ]

    orb_in = [
        send(
            remote(orb.at[:, :, pl.ds(0, LANES)], yhi, ORB_Y, ORB_Y, neighbour(0, -1, 0)), has_ylo, has_yhi
        ),
        send(
            remote(orb.at[:, :, pl.ds(YZ - LANES, LANES)], ylo, ORB_Y + 1, ORB_Y + 1, neighbour(0, 1, 0)),
            has_yhi, has_ylo,
        ),
        send(remote(orb, zbuf, ORB_Z, ORB_Z, neighbour(0, 0, 1)), None, None),
    ]
    orb_x_in = orbitals_along_x(0)

    def zero(ref, *index):
        def run():
            view = ref.at[index] if index else ref
            view[...] = jnp.zeros(view.shape, view.dtype)
        return run

    when(jnp.logical_not(has_xhi), zero(xhi))
    when(jnp.logical_not(has_xlo), zero(xlo))
    for ref in (edge_v, edge_c):
        when(jnp.logical_not(has_xhi), zero(ref, 0))
        when(jnp.logical_not(has_xlo), zero(ref, 1))
    when(jnp.logical_not(has_ylo), zero(ylo))
    when(jnp.logical_not(has_yhi), zero(yhi))
    for dx, dy, dz in OFFSETS:
        cond = exists(dx, dy)
        if cond is not None:
            when(jnp.logical_not(cond), zero(rh, slot_of(dx, dy, dz)))
    for side, dy in ((0, -1), (1, 1)):
        for dx in (-1, 0, 1):
            when(jnp.logical_not(exists(-dx, -dy)), zero(rim_in, 1 - dx, side))
    for x in range(NX):
        for ref in (va, vb, sa):
            ref[x, 0:Y0, :] = jnp.zeros((Y0, LANES), F32)
            ref[x, Y0 + FY :, :] = jnp.zeros((Y0, LANES), F32)
    cbuf[...] = jnp.zeros(cbuf.shape, F32)
    xo[...] = jnp.zeros(xo.shape, F32)
    xz[...] = jnp.zeros(xz.shape, F32)

    def fill_w(r, carry):
        row = iota((LANES, 384), 0) + r * LANES
        col = iota((LANES, 384), 1)
        place = iota((1, 384), 1) % BZ
        diff = row - LANES - col
        main = jnp.where(diff == 0, 3.0, 0.0)
        side = (
            (diff == BZ) | (diff == -BZ)
            | ((diff == 1) & (place != BZ - 1)) | ((diff == -1) & (place != 0))
        )
        main = jnp.where(side, -0.5, main)
        far = row - 640 - col
        over = jnp.where(
            bk == 0,
            jnp.where((far == 1 - BZ) & (place == BZ - 1), -0.5, 0.0),
            jnp.where((far == BZ - 1) & (place == 0), -0.5, 0.0),
        )
        w_ref[pl.ds(pl.multiple_of(r * LANES, LANES), LANES), :] = jnp.where(row < 640, main, over).astype(BF16)
        return carry

    lax.fori_loop(0, 8, fill_w, 0)

    lane12 = iota((12, LANES), 1)

    def thread(a0, a1, a2, lanes):
        y0 = a0
        y1 = jnp.where(lanes < 32, pltpu.roll(a0, 32, 1), pltpu.roll(a1, 32, 1))
        y2 = jnp.where(lanes < 64, pltpu.roll(a1, 64, 1), pltpu.roll(a2, 64, 1))
        y3 = pltpu.roll(a2, 96, 1)
        return [jnp.where(lanes < FZ, val, 0.0) for val in (y0, y1, y2, y3)]

    fields = ((pvx, va, 1.0), (cmx, sa, -math.pi))

    def split(x):
        base = EDGE - 36 * M + 36 * x
        for src, dst, scale in fields:
            rows = [scale * src[pl.ds(base + r, 12, stride=3), :] for r in range(3)]
            for q, val in enumerate(thread(*rows, lane12)):
                dst[x, pl.ds(Y0 + q, 12, stride=4), :] = val

    loop(M, M + FX, split, 6)

    arrive(*band_in)
    rho = gath[0].astype(F32)
    for d in range(1, n_band):
        rho = rho + gath[d].astype(F32)
    rho = jnp.where(iota((8, YZ), 0) < BX, unpacked(rho), 0.0)
    tot[...] = rho
    totb[...] = packed(rho)
    halo_in = []
    for dx, dy, dz in sorted(OFFSETS, key=lambda o: (-abs(o[0]) - abs(o[1]), -abs(o[0]), -o[2])):
        there = slot_of(-dx, -dy, dz)
        cols = {0: pl.ds(0, YZ), -1: pl.ds(0, 256), 1: pl.ds(YZ - 256, 256)}[dy]
        cp = remote(
            totb.at[:, cols], rh.at[there, :, cols], HALO + slot_of(dx, dy, dz), HALO + there,
            neighbour(dx, dy, dz),
        )
        halo_in.append(send(cp, exists(dx, dy), exists(-dx, -dy)))

    orb_x_in = orb_x_in + orbitals_along_x(1)

    arrive(*px_in)
    for full, edge in ((pvx, edge_v), (cmx, edge_c)):
        full[EDGE + OWN : 2 * EDGE + OWN, :] = edge[0].astype(F32)
        full[0:EDGE, :] = edge[1].astype(F32)
    loop(0, M, split, 5)
    loop(M + FX, NX, split, 5)
    arrive(*rim_copies)
    lane22 = iota((NX, LANES), 1)
    for n, (_, dst, scale) in enumerate(fields):
        flat = dst.reshape((NX + 2) * YROWS, LANES)
        for side in range(2):
            rim_tmp[0, 0, 0:20, :] = rim_in[0, side, n].astype(F32)[28:48]
            rim_tmp[0, 0, 20:48, :] = rim_in[1, side, n].astype(F32)[0:28]
            rim_tmp[0, 1, 0:20, :] = rim_in[1, side, n].astype(F32)[28:48]
            rim_tmp[0, 1, 20:40, :] = rim_in[2, side, n].astype(F32)[0:20]
            rim_all[side, n, 0:48, :] = rim_tmp[0, 0, 0:48, :]
            rim_all[side, n, 48:88, :] = rim_tmp[0, 1, 0:40, :]
            a = [scale * rim_all[side, n, pl.ds(r, NX, stride=4), :] for r in range(4)]
            if side == 0:
                cells = [*thread(a[0], a[1], a[2], lane22), jnp.where(lane22 < FZ, a[3], 0.0)]
                first = Y0 + FY
            else:
                cells = [jnp.where(lane22 < FZ, pltpu.roll(a[0], 96, 1), 0.0), *thread(a[1], a[2], a[3], lane22)]
                first = Y0 - M
            for q, val in enumerate(cells):
                flat[pl.ds(first + q, NX, stride=YROWS), :] = val

    lane = iota((SPAN, LANES), 1)
    span = slice(Y0 - 8, Y0 - 8 + SPAN)
    inner = (lane < M) | ((lane >= 64) & (lane < 64 + M))

    def pack_z(x):
        v, s = va[x, span, :], sa[x, span, :]
        first = jnp.where(lane < 64, v, pltpu.roll(s, 64, 1))
        last = jnp.where(lane < 64, pltpu.roll(v, 16 + M - FZ + LANES, 1), pltpu.roll(s, 80 + M - FZ + LANES, 1))
        zsend[x] = jnp.where(inner, first, last).astype(BF16)

    loop(0, NX, pack_z, 11)
    z_in = send(remote(zsend, zrecv, POT_Z, POT_Z, neighbour(0, 0, 1)), None, None)

    for x in range(BX):
        base[x : x + 1, :] = loc[x]
    base[...] = base[...] - jnp.exp(jnp.log((3.0 / math.pi) * tot[...]) * (1.0 / 3.0))

    arrive(*orb_in)
    for first in (0, 3):
        group = slice(first, first + 3)
        for t in range(3):
            if t == 0:
                here = [ylo[group], waves[group, :, 0:512]]
            elif t == 1:
                here = [waves[group, :, 256:896]]
            else:
                here = [waves[group, :, 640:1152], yhi[group]]
            cols = slice(384 * t, 384 * (t + 1))
            lhs = jnp.concatenate([*here, zbuf[group, :, cols]], 2).reshape(3 * nb, 1024)
            out = jnp.dot(lhs, w_ref[...], preferred_element_type=F32).reshape(3, nb, 384)
            for u in range(3):
                x = first + u
                sides = [waves[other, :, cols].astype(F32) for other in (x - 1, x + 1) if 0 <= other < BX]
                stencil[x, :, cols] = out[u] - 0.5 * sum(sides[1:], sides[0])

    arrive(z_in)
    from_z = jnp.where(bk == 0, jnp.where((lane >= FZ) & (lane < FZ + M), 1, 0), jnp.where(lane >= LANES - M, 1, 0)) == 1
    shift_v = jnp.where(bk == 0, FZ, LANES - M - 16)
    shift_s = jnp.where(bk == 0, FZ - 64, 64 - M - 16)

    def merge(x):
        rim = zrecv[x].astype(F32)
        va[x, span, :] = jnp.where(from_z, pltpu.roll(rim, shift_v, 1), va[x, span, :])
        sa[x, span, :] = jnp.where(from_z, pltpu.roll(rim, shift_s, 1), sa[x, span, :])

    loop(0, NX, merge, 11)


    arrive(*halo_in)
    for dst, dz in ((xo, 0), (xz, 1)):
        for dy, start, width, at in ((0, 0, YZ, 256), (-1, YZ - 256, 256, 0), (1, 0, 256, 256 + YZ)):
            cols = slice(start, start + width)
            own = tot[...] if dz == 0 and dy == 0 else unpacked(rh[slot_of(0, dy, dz), :, cols].astype(F32))
            above = unpacked(rh[slot_of(1, dy, dz), :, cols].astype(F32))
            below = unpacked(rh[slot_of(-1, dy, dz), :, cols].astype(F32))
            lanes = slice(at, at + width)
            dst[0:3, lanes] = below[3:6]
            dst[3:9, lanes] = own[0:6]
            dst[9:12, lanes] = above[0:3]

    def split_rho(g):
        window = pl.ds(pl.multiple_of(g * 384, 384), 512)
        for src, base in ((xo, 0), (xz, 64)):
            block = src[:, window]
            for q in range(8):
                cbuf[g * 8 + q, :, base : base + BZ] = block[:, 112 + BZ * q : 112 + BZ * (q + 1)]

    loop(0, 4, split_rho, 4)
    source_row = iota((LANES, LANES), 0)
    fine_lane = iota((LANES, LANES), 1)
    fine_z = jnp.where(fine_lane >= LANES - M, fine_lane - LANES, fine_lane)
    coarse = jnp.where(source_row < 64, source_row, source_row - 64 + jnp.where(bk == 0, BZ, -BZ))
    real = (source_row < BZ) | ((source_row >= 64) & (source_row < 64 + BZ))
    odd = (fine_z + 128) % 2
    floor = (fine_z + 128) // 2 - 64
    wz = jnp.where(coarse == floor, 0.75 * math.pi, 0.0)
    wz = jnp.where(coarse == floor - 1 + 2 * odd, 0.25 * math.pi, wz)
    wz = jnp.where(real, wz, 0.0)
    fine = jnp.dot(
        cbuf[...].reshape(32 * 16, LANES), wz, precision=EXACT, preferred_element_type=F32
    ).reshape(32, 16, LANES)
    for y in range(30):
        f1[pl.ds(y + 5, 12, stride=40), :] = fine[y, 0:12]

    def refine_y(x):
        base = pl.multiple_of(x * 40, 8)
        block = f1[pl.ds(base, 40), :]
        mid = 0.75 * block[6:34]
        f2[x, pl.ds(4, 28, stride=2), :] = mid + 0.25 * block[5:33]
        f2[x, pl.ds(5, 28, stride=2), :] = mid + 0.25 * block[7:35]

    loop(0, 12, refine_y, 12)

    def refine_x(x):
        mid = 0.75 * f2[x, 0:SPAN, :]
        at = 2 * x - 1
        sa[at, span, :] = sa[at, span, :] + mid + 0.25 * f2[x - 1, 0:SPAN, :]
        sa[at + 1, span, :] = sa[at + 1, span, :] + mid + 0.25 * f2[x + 1, 0:SPAN, :]

    loop(1, 11, refine_x, 10)

    yrow = iota((SPAN, LANES), 0)
    y_ok = ((yrow >= 8) | has_ylo) & ((yrow < 8 + FY) | has_yhi)
    z_ok = (lane < FZ) | from_z
    sixth = jnp.where(y_ok & z_ok, 1.0 / 6.0, 0.0)
    x_low = jnp.where(has_xlo, 1.0, 0.0)
    x_high = jnp.where(has_xhi, 1.0, 0.0)

    for sweep in range(SWEEPS):
        old, new = (va, vb) if sweep % 2 == 0 else (vb, va)

        def update(x, old=old, new=new):
            mid = old[x, span, :]
            acc = old[x - 1, span, :] + old[x + 1, span, :] + sa[x, span, :]
            acc = acc + (old[x, Y0 - 9 : Y0 - 9 + SPAN, :] + old[x, Y0 - 7 : Y0 - 7 + SPAN, :])
            acc = acc + pltpu.roll(mid, 1, 1) + pltpu.roll(mid, LANES - 1, 1)
            factor = sixth
            if x < M:
                factor = sixth * x_low
            elif x >= M + FX:
                factor = sixth * x_high
            new[x, span, :] = acc * factor

        loop(1 + sweep, NX - 1 - sweep, update, NX - 2 - 2 * sweep)

    arrive(*orb_x_in)
    stencil[0] = stencil[0] - 0.5 * xlo[...].astype(F32)
    stencil[BX - 1] = stencil[BX - 1] - 0.5 * xhi[...].astype(F32)

    for x in range(BX):
        at = 2 * x + M
        g3[x, 0:YROWS, :] = 0.125 * (va[at - 1] + va[at + 2]) + 0.375 * (va[at] + va[at + 1])
    for x in range(BX):
        c3[BY * x : BY * (x + 1), :] = 0.125 * (
            g3[x, pl.ds(Y0 - 1, BY, stride=2), :] + g3[x, pl.ds(Y0 + 2, BY, stride=2), :]
        ) + 0.375 * (g3[x, pl.ds(Y0, BY, stride=2), :] + g3[x, pl.ds(Y0 + 1, BY, stride=2), :])
    lane_in = iota((LANES, LANES), 0)
    cell = iota((LANES, LANES), 1)
    rel = jnp.where(lane_in == LANES - 1, -1, lane_in) - 2 * cell
    wr = jnp.where((rel == 0) | (rel == 1), 0.375, 0.0)
    wr = jnp.where((rel == -1) | (rel == 2), 0.125, wr)
    wr = jnp.where(cell < BZ, wr, 0.0)
    c3[0 : BX * BY, :] = jnp.dot(c3[0 : BX * BY, :], wr, precision=EXACT, preferred_element_type=F32)
    for y in range(BY):
        tmp_m[0:BX, y * BZ : (y + 1) * BZ] = c3[pl.ds(y, BX, stride=BY), :][:, 0:BZ]
    eff_out[...] = tmp_m[0:BX, :] + base[0:BX, :]

    def join(x):
        p0, p1, p2, p3 = (va[x + M, pl.ds(Y0 + q, 12, stride=4), :] for q in range(4))
        r0 = jnp.where(lane12 < 96, p0, pltpu.roll(p1, 96, 1))
        r1 = jnp.where(lane12 < 64, pltpu.roll(p1, 96, 1), pltpu.roll(p2, 64, 1))
        r2 = jnp.where(lane12 < 32, pltpu.roll(p2, 64, 1), pltpu.roll(p3, 32, 1))
        for r, val in enumerate((r0, r1, r2)):
            pot_out[pl.ds(36 * x + r, 12, stride=3), :] = val

    loop(0, FX, join, 6)

    finish()


def apply_kernel(stencil, effective, waves, potential, applied_out, potential_out, applied, sem):
    cp_pot = pltpu.make_async_copy(potential.at[pl.ds(0, OWN)], potential_out, sem.at[BX])
    cp_pot.start()
    copies = []
    for x in range(BX):
        here = stencil[x] + effective[x : x + 1, :] * waves[x].astype(F32)
        applied[x] = here.astype(BF16)
        cp = pltpu.make_async_copy(applied.at[x], applied_out.at[x], sem.at[x])
        cp.start()
        copies.append(cp)
    for cp in copies:
        cp.wait()
    cp_pot.wait()


def solution(mesh):
    n_band = mesh.shape["band"]
    domains = mesh.shape["dom"]
    ny = min(4, domains // 4)
    nx = domains // (ny * 2)

    def local(orbitals, occupations, previous, compensation, local_potential):
        nb = orbitals.shape[0]
        hbm = pl.BlockSpec(memory_space=pltpu.HBM)
        vmem = pl.BlockSpec(memory_space=pltpu.VMEM)
        waves = orbitals[:, 0].transpose(1, 0, 2)
        stencil, effective, potential, held = pl.pallas_call(
            functools.partial(step_kernel, (nb, n_band, nx, ny)),
            out_shape=(
                jax.ShapeDtypeStruct((BX, nb, YZ), F32),
                jax.ShapeDtypeStruct((BX, YZ), F32),
                jax.ShapeDtypeStruct((OWN + 16, LANES), F32),
                jax.ShapeDtypeStruct((BX, nb, YZ), BF16),
            ),
            in_specs=[hbm] * 5,
            out_specs=(vmem,) * 4,
            scratch_shapes=[
                pltpu.VMEM((nb, YZ), BF16),
                pltpu.VMEM((nb, YZ), BF16),
                pltpu.VMEM((BX, nb, YZ), BF16),
                pltpu.VMEM((BX, nb, LANES), BF16),
                pltpu.VMEM((BX, nb, LANES), BF16),
                pltpu.VMEM((1024, 384), BF16),
                pltpu.VMEM((1, nb), F32),
                pltpu.VMEM((nb, LANES), F32),
                pltpu.VMEM((2 * EDGE + OWN, LANES), F32),
                pltpu.VMEM((2 * EDGE + OWN, LANES), F32),
                pltpu.VMEM((OWN, LANES), BF16),
                pltpu.VMEM((OWN, LANES), BF16),
                pltpu.VMEM((2, EDGE, LANES), BF16),
                pltpu.VMEM((2, EDGE, LANES), BF16),
                pltpu.VMEM((BX, 1, YZ), F32),
            ]
            + [pltpu.VMEM((NX + 2, YROWS, LANES), F32)] * 3
            + [
                pltpu.VMEM((2, 2, 56, LANES), F32),
                pltpu.VMEM((2, 2, 48, LANES), BF16),
                pltpu.VMEM((3, 2, 2, 48, LANES), BF16),
                pltpu.VMEM((2, 2, 96, LANES), F32),
                pltpu.VMEM((NX, SPAN, LANES), BF16),
                pltpu.VMEM((NX, SPAN, LANES), BF16),
                pltpu.VMEM((8, YZ), F32),
                pltpu.VMEM((n_band, 8, YZ), BF16),
                pltpu.VMEM((8, YZ), F32),
                pltpu.VMEM((8, YZ), BF16),
                pltpu.VMEM((18, 8, YZ), BF16),
                pltpu.VMEM((16, 512 + YZ), F32),
                pltpu.VMEM((16, 512 + YZ), F32),
                pltpu.VMEM((32, 16, LANES), F32),
                pltpu.VMEM((16 * 40, LANES), F32),
                pltpu.VMEM((12, SPAN + 8, LANES), F32),
                pltpu.VMEM((BX, YROWS, LANES), F32),
                pltpu.VMEM((8 * BY, LANES), F32),
                pltpu.VMEM((8, YZ), F32),
                pltpu.VMEM((8, YZ), F32),
                pltpu.SemaphoreType.DMA((BX + 4,)),
                pltpu.SemaphoreType.DMA((N_SEM,)),
                pltpu.SemaphoreType.DMA((N_SEM,)),
            ],
            compiler_params=pltpu.CompilerParams(
                collective_id=0, has_side_effects=True, vmem_limit_bytes=48 * 1024 * 1024
            ),
        )(
            pltpu.with_memory_space_constraint(waves, pltpu.HBM),
            pltpu.with_memory_space_constraint(occupations.reshape(1, nb), pltpu.HBM),
            pltpu.with_memory_space_constraint(previous.reshape(OWN, LANES), pltpu.HBM),
            pltpu.with_memory_space_constraint(compensation.reshape(OWN, LANES), pltpu.HBM),
            pltpu.with_memory_space_constraint(local_potential.reshape(BX, 1, YZ), pltpu.HBM),
        )
        applied, potential = pl.pallas_call(
            apply_kernel,
            out_shape=(
                jax.ShapeDtypeStruct((BX, nb, YZ), BF16),
                jax.ShapeDtypeStruct((OWN, LANES), F32),
            ),
            in_specs=[vmem] * 4,
            out_specs=(hbm, hbm),
            scratch_shapes=[pltpu.VMEM((BX, nb, YZ), BF16), pltpu.SemaphoreType.DMA((BX + 1,))],
            compiler_params=pltpu.CompilerParams(vmem_limit_bytes=8 * 1024 * 1024),
        )(stencil, effective, held, potential)
        return applied.transpose(1, 0, 2)[:, None], potential.reshape(previous.shape)

    return jax.shard_map(
        local,
        mesh=mesh,
        in_specs=(
            P("band", "dom", None, None),
            P("band"),
            P("dom", None, None),
            P("dom", None, None),
            P("dom", None, None),
        ),
        out_specs=(P("band", "dom", None, None), P("dom", None, None)),
        check_vma=False,
    )
```
